128 devices in a mesh: row: 8 (over z, core), col: 16 (over x, y).
Axes of the slice: x: 4, y: 4, z: 4, core: 2. Of those that a mesh axis runs over, the one named last changes fastest.
Arguments:
- images: bfloat16 [8, 64, 65536], P(None, 'row', 'col'), may hold values from -6 to 6
- kernel: bfloat16 [3, 3, 1024, 1024], P(None, None, 'col', 'row'), may hold values from -0.09375 to 0.09375
- upstream: bfloat16 [8, 64, 65536], P(None, 'row', 'col'), may hold values from -6 to 6
Outputs:
- output_maps: bfloat16 [8, 64, 65536], P(None, 'row', 'col')
- input_grad: bfloat16 [8, 64, 65536], P(None, 'row', 'col')
- kernel_grad: float32 [3, 3, 1024, 1024], P(None, None, 'col', 'row')
The draws below stay inside these ranges and needn't reach their ends.
All inputs are finite; a program needn't handle non-finite values.
Results may differ from the reference program's by a relative error of at most 0.001.
Values may be sent and summed in bfloat16 or wider, within the bound.
No kernel may reach another device: no remote copies, remote signals or barrier semaphores. Data moves between devices by JAX's collectives and lax.ppermute only.
A program may use at most 128 MiB of HBM per device.

```python
import jax
import jax.numpy as jnp
from jax import lax

CIN = 1024
COUT = 1024
W = 64
IMAGES = 8
H = 64


def with_spikes(array, own_key, source, target, shards_of, factor):
    owner, partner = [(jnp.arange(array.shape[dim]) // (array.shape[dim] // shards_of)).reshape([-1 if axis == dim else 1 for axis in range(array.ndim)]) for dim in (source, target)]
    chosen = jax.random.permutation(own_key, shards_of)[partner]
    strong = (owner == chosen) | (owner == (partner + shards_of // 2) % shards_of)
    return jnp.where(strong, factor * array, array)


def shard_levels(stream_key, extent, cuts, smallest, largest):
    loudness, own = 1.0, jax.random.fold_in(stream_key, 6)
    for position, parts in cuts:
        steps = jnp.exp(jax.random.uniform(jax.random.fold_in(own, position), (parts,), jnp.float32, smallest / len(cuts), largest / len(cuts)))
        loudness = loudness * jnp.repeat(steps, extent[position] // parts).reshape([-1 if axis == position else 1 for axis in range(len(extent))])
    return loudness


def normal_values(stream_key, shape, scale, bound, split=(), kind=jnp.bfloat16):
    level = shard_levels(stream_key, shape, split, -0.22, 0.18) if split else 1.0
    drawn = jax.random.normal(stream_key, shape, jnp.float32) * scale * level
    return jnp.minimum(jnp.maximum(drawn, -bound), bound).astype(kind)


def bell_draw_with(key, shape, spread, most, pieces, heavy, dtype=jnp.bfloat16):
    result = spread * jax.random.normal(key, shape, jnp.float32)
    if pieces:
        result = result * shard_levels(key, shape, pieces, -0.22, 0.18)
    return jnp.clip(with_spikes(result, jax.random.fold_in(key, 3), *heavy), -most, most).astype(dtype)


def setup_inputs(seed: int = 0) -> dict:
    seeds = jax.random.split(jax.random.key(seed), 4)
    return {
        "images": bell_draw_with(seeds[0], (IMAGES, H, CIN * W), 1.0, 6.0, ((1, 8), (2, 16)), (1, 2, 16, 2.0)),
        "kernel": bell_draw_with(seeds[1], (3, 3, COUT, CIN), (9 * CIN) ** -0.5, 0.09375, ((2, 16), (3, 8)), (2, 3, 16, 2.0)),
        "upstream": normal_values(seeds[2], (IMAGES, H, COUT * W), 1.0, 6.0, ((1, 8), (2, 16))),
    }


def convolve(inputs, weights):
    return lax.conv_general_dilated(inputs.astype(jnp.float32), weights.astype(jnp.float32), (1, 1), ((1, 1), (1, 1)), dimension_numbers=("NHWC", "HWIO", "NHWC"), precision=lax.Precision.HIGHEST)


def to_maps(flat, channels):
    return flat.reshape(flat.shape[0], flat.shape[1], channels, W).transpose(0, 1, 3, 2)


def to_flat(maps):
    return maps.transpose(0, 1, 3, 2).reshape(maps.shape[0], maps.shape[1], maps.shape[3] * maps.shape[2])


def reference(images, kernel, upstream):
    inputs = to_maps(images, CIN)
    gradient_maps = to_maps(upstream, COUT)
    hwio = kernel.transpose(0, 1, 3, 2)
    output_maps = to_flat(convolve(inputs, hwio)).astype(jnp.bfloat16)
    turned = jnp.flip(kernel, (0, 1))
    input_grad = to_flat(convolve(gradient_maps, turned)).astype(jnp.bfloat16)
    padded = jnp.pad(inputs.astype(jnp.float32), ((0, 0), (1, 1), (1, 1), (0, 0)))
    gradient = gradient_maps.astype(jnp.float32)
    height = inputs.shape[1]
    width = inputs.shape[2]
    rows_list = []
    for tap_row in range(3):
        cols_list = []
        for tap_col in range(3):
            window = padded[:, tap_row:tap_row + height, tap_col:tap_col + width, :]
            cols_list.append(jnp.einsum("bhwi,bhwo->oi", window, gradient, precision=lax.Precision.HIGHEST))
        rows_list.append(jnp.stack(cols_list))
    kernel_grad = jnp.stack(rows_list)
    return output_maps, input_grad, kernel_grad
```

```python
import functools

import jax
import jax.numpy as jnp
from jax import lax
from jax.experimental import pallas as pl
from jax.experimental.pallas import tpu as pltpu
from jax.sharding import Mesh, PartitionSpec as P

W = 64
LANES = 128
F32 = jnp.float32
BF16 = jnp.bfloat16
STEPS = (0, 1, 3, 2)
VMEM_LIMIT = 60 * 1024 * 1024


def params():
    return pltpu.CompilerParams(vmem_limit_bytes=VMEM_LIMIT)


def lane_of(shape):
    return lax.broadcasted_iota(jnp.int32, shape, len(shape) - 1)


def slot_rows(position, step):
    return pl.multiple_of(lax.rem(position + step, 4) * 64, 64)


def pack_kernel(x_ref, o_ref, rows_ref, mix_ref):
    pairs = x_ref.shape[0] // 2
    low = lane_of((32, LANES)) < W
    for q in range(pairs):
        for side in range(2):
            flat = x_ref[q + pairs * side].astype(F32)
            for p in range(32):
                rows_ref[side, :, p, :] = flat[:, p * LANES : (p + 1) * LANES]
        for h in range(8):
            first = rows_ref[0, h]
            second = rows_ref[1, h]
            even = jnp.where(low, first, pltpu.roll(second, W, 1))
            odd = jnp.where(low, pltpu.roll(first, W, 1), second)
            mix_ref[h, pl.ds(0, 32, stride=2), :] = even
            mix_ref[h, pl.ds(1, 32, stride=2), :] = odd
        for h in range(8):
            o_ref[q, :, h * LANES : (h + 1) * LANES] = mix_ref[h].astype(BF16)


def pack(x):
    return pl.pallas_call(
        pack_kernel,
        out_shape=jax.ShapeDtypeStruct((4, 64, 1024), BF16),
        in_specs=[pl.BlockSpec(memory_space=pltpu.VMEM)],
        out_specs=pl.BlockSpec(memory_space=pltpu.VMEM),
        scratch_shapes=[pltpu.VMEM((2, 8, 32, LANES), F32), pltpu.VMEM((8, 64, LANES), F32)],
        compiler_params=params(),
        name="pack",
    )(x)


def finish_kernel(own_a, own_b, ma, mb, pa, pb, o_ref, mix_ref, rows_ref):
    low = lane_of((32, LANES)) < W
    for q in range(4):
        half = q // 2
        j = q % 2
        own, minus, plus = ((own_a, ma, pa), (own_b, mb, pb))[half]
        for h in range(8):
            lanes = slice(h * LANES, (h + 1) * LANES)
            mix_ref[h] = own[j, :, lanes] + minus[j, :, lanes] + plus[j, :, lanes]
        for h in range(8):
            even = mix_ref[h, pl.ds(0, 32, stride=2), :]
            odd = mix_ref[h, pl.ds(1, 32, stride=2), :]
            rows_ref[0, h] = jnp.where(low, even, pltpu.roll(odd, W, 1))
            rows_ref[1, h] = jnp.where(low, pltpu.roll(even, W, 1), odd)
        for side in range(2):
            for p in range(32):
                o_ref[q + 4 * side, :, p * LANES : (p + 1) * LANES] = rows_ref[side, :, p, :].astype(BF16)


def finish(*pieces):
    return pl.pallas_call(
        finish_kernel,
        out_shape=jax.ShapeDtypeStruct((8, 8, 4096), BF16),
        in_specs=[pl.BlockSpec(memory_space=pltpu.VMEM)] * 6,
        out_specs=pl.BlockSpec(memory_space=pltpu.VMEM),
        scratch_shapes=[pltpu.VMEM((8, 64, LANES), F32), pltpu.VMEM((2, 8, 32, LANES), F32)],
        compiler_params=params(),
        name="finish",
    )(*pieces)


def weights_kernel(at, mine, other, w_ref, wt_ref, whole, turned):
    z, c, x, y = at[0], at[1], at[2], at[3]
    near = pl.multiple_of(c * LANES, LANES)
    far = pl.multiple_of((1 - c) * LANES, LANES)
    for j in range(4):
        rows = slot_rows(z, 4 - j)
        for tap in range(9):
            whole[tap, pl.ds(rows, 64), pl.ds(near, LANES)] = mine[j, tap]
            whole[tap, pl.ds(rows, 64), pl.ds(far, LANES)] = other[j, tap]
    one = jnp.where(
        lax.broadcasted_iota(jnp.int32, (256, 256), 0) == lax.broadcasted_iota(jnp.int32, (256, 256), 1), 1.0, 0.0
    ).astype(BF16)
    for tap in range(9):
        turned[tap] = lax.dot_general(
            one, whole[tap], (((1,), (1,)), ((), ())), preferred_element_type=F32
        ).astype(BF16)
    for k, step in enumerate(STEPS):
        for tap in range(9):
            w_ref[tap, k * 64 : (k + 1) * 64, :] = whole[tap, pl.ds(slot_rows(x, step), 64), :]
            wt_ref[tap, k * 64 : (k + 1) * 64, :] = turned[tap, pl.ds(slot_rows(y, step), 64), :]


def arrange_weights(at, mine, other):
    shape = jax.ShapeDtypeStruct((9, 256, 256), BF16)
    return pl.pallas_call(
        weights_kernel,
        out_shape=(shape, shape),
        in_specs=[pl.BlockSpec(memory_space=pltpu.SMEM)] + [pl.BlockSpec(memory_space=pltpu.VMEM)] * 2,
        out_specs=[pl.BlockSpec(memory_space=pltpu.VMEM)] * 2,
        scratch_shapes=[pltpu.VMEM((9, 256, 256), BF16)] * 2,
        compiler_params=params(),
        name="weights",
    )(at, mine, other)


def lay_shifted(position, chunks, top, bottom, shifted):
    lane = lane_of((64, LANES)) % W
    for k, step in enumerate(STEPS):
        rows = pl.ds(slot_rows(position, step), 64)
        for h in range(10):
            if h == 0:
                tile = top[k, 0]
            elif h == 9:
                tile = bottom[k, 0]
            else:
                tile = chunks[k][0, :, (h - 1) * LANES : h * LANES]
            wide = tile.astype(F32)
            lanes = slice(h * LANES, (h + 1) * LANES)
            shifted[0, rows, lanes] = jnp.where(lane == 0, 0.0, pltpu.roll(wide, 1, 1)).astype(BF16)
            shifted[1, rows, lanes] = tile
            shifted[2, rows, lanes] = jnp.where(lane == W - 1, 0.0, pltpu.roll(wide, LANES - 1, 1)).astype(BF16)


def conv_kernel(which, flip, at, c0, c1, c2, c3, top, bottom, w_ref, o0, o1, o2, o3, shifted):
    lay_shifted(at[which], (c0, c1, c2, c3), top, bottom, shifted)
    for n in range(4):
        total = None
        for a in range(3):
            for c in range(3):
                tap = (2 - a) * 3 + (2 - c) if flip else a * 3 + c
                start = a * LANES + n * 256
                part = jnp.dot(w_ref[tap], shifted[c, :, start : start + 256], preferred_element_type=F32)
                total = part if total is None else total + part
        for k, o_ref in enumerate((o0, o1, o2, o3)):
            o_ref[0, :, n * 256 : (n + 1) * 256] = total[k * 64 : (k + 1) * 64]


def conv(which, flip, first, at, chunks, top, bottom, weights):
    shape = jax.ShapeDtypeStruct((2, 64, 1024), F32)
    chunk = pl.BlockSpec((1, 64, 1024), lambda q: (q + first, 0, 0))
    edge = pl.BlockSpec((4, 1, 64, LANES), lambda q: (0, q + first, 0, 0))
    return pl.pallas_call(
        functools.partial(conv_kernel, which, flip),
        out_shape=(shape,) * 4,
        grid=(2,),
        in_specs=[pl.BlockSpec(memory_space=pltpu.SMEM)]
        + [chunk] * 4
        + [edge] * 2
        + [pl.BlockSpec((9, 256, 256), lambda q: (0, 0, 0))],
        out_specs=[pl.BlockSpec((1, 64, 1024), lambda q: (q, 0, 0))] * 4,
        scratch_shapes=[pltpu.VMEM((3, 256, 1280), BF16)],
        compiler_params=params(),
        cost_estimate=pl.CostEstimate(flops=2415919104, bytes_accessed=6000000, transcendentals=0),
        name="conv_grad" if flip else "conv_out",
    )(at, *chunks, top, bottom, weights)


def kernel_grad_kernel(at, x0, x1, x2, x3, top, bottom, g0, g1, g2, g3, mine, other, shifted, grads, total):
    z, core, x, y = at[0], at[1], at[2], at[3]
    q = pl.program_id(0)
    lay_shifted(y, (x0, x1, x2, x3), top, bottom, shifted)
    for k, step in enumerate(STEPS):
        grads[pl.ds(slot_rows(x, step), 64), :] = (g0, g1, g2, g3)[k][0]

    @pl.when(q == 0)
    def _():
        total[...] = jnp.zeros_like(total)

    for a in range(3):
        for c in range(3):
            total[a * 3 + c] += lax.dot_general(
                grads[...],
                shifted[c, :, a * LANES : a * LANES + 1024],
                (((1,), (1,)), ((), ())),
                preferred_element_type=F32,
            )

    @pl.when(q == 3)
    def _():
        near = pl.multiple_of(core * LANES, LANES)
        far = pl.multiple_of((1 - core) * LANES, LANES)
        for k, step in enumerate(STEPS):
            rows = pl.ds(slot_rows(z, step), 64)
            for tap in range(9):
                mine[k, tap] = total[tap, rows, pl.ds(near, LANES)]
                other[k, tap] = total[tap, rows, pl.ds(far, LANES)]


def weight_grads(at, chunks, top, bottom, grads):
    shape = jax.ShapeDtypeStruct((4, 9, 64, LANES), F32)
    chunk = pl.BlockSpec((1, 64, 1024), lambda q: (q, 0, 0))
    edge = pl.BlockSpec((4, 1, 64, LANES), lambda q: (0, q, 0, 0))
    whole = pl.BlockSpec((4, 9, 64, LANES), lambda q: (0, 0, 0, 0))
    return pl.pallas_call(
        kernel_grad_kernel,
        out_shape=(shape,) * 2,
        grid=(4,),
        in_specs=[pl.BlockSpec(memory_space=pltpu.SMEM)] + [chunk] * 4 + [edge] * 2 + [chunk] * 4,
        out_specs=[whole] * 2,
        scratch_shapes=[
            pltpu.VMEM((3, 256, 1280), BF16),
            pltpu.VMEM((256, 1024), BF16),
            pltpu.VMEM((9, 256, 256), F32),
        ],
        compiler_params=params(),
        cost_estimate=pl.CostEstimate(flops=4831838208, bytes_accessed=9000000, transcendentals=0),
        name="weight_grads",
    )(at, *chunks, top, bottom, *grads)


def ring(step):
    return [(i, (i + step) % 4) for i in range(4)]


def gather(block, axis):
    return (
        block,
        lax.ppermute(block, axis, ring(3)),
        lax.ppermute(block, axis, ring(1)),
        lax.ppermute(block, axis, ring(2)),
    )


def edges(chunks):
    forward = [(i, i + 1) for i in range(7)]
    backward = [(j, i) for i, j in forward]
    last = jnp.stack([chunk[:, :, -LANES:] for chunk in chunks])
    first = jnp.stack([chunk[:, :, :LANES] for chunk in chunks])
    return lax.ppermute(last, ("z", "core"), forward), lax.ppermute(first, ("z", "core"), backward)


def reduce_to_owner(part_a, part_b, axis):
    own_a, next_a, prev_a, far_a = part_a
    own_b, next_b, prev_b, far_b = part_b
    up, down = ring(1), ring(3)
    relay_a = lax.ppermute(far_a, axis, up)
    relay_b = lax.ppermute(far_b, axis, down)
    from_prev_b = lax.ppermute(next_b, axis, up)
    from_next_a = lax.ppermute(prev_a, axis, down)
    from_prev_a = lax.ppermute(next_a + relay_a, axis, up)
    from_next_b = lax.ppermute(prev_b + relay_b, axis, down)
    return finish(own_a, own_b, from_prev_a, from_prev_b, from_next_a, from_next_b)


def shards(images, kernel, upstream):
    at = jnp.stack([lax.axis_index(n) for n in ("z", "core", "x", "y")]).astype(jnp.int32)
    x_chunks = gather(pack(images), "y")
    g_chunks = gather(pack(upstream), "x")

    block = kernel.reshape(9, 64, LANES)
    mine = []
    for j in range(4):
        pairs = [(z * 4 + x, ((x + j) % 4) * 4 + z) for z in range(4) for x in range(4)]
        mine.append(lax.ppermute(block, ("z", "x"), pairs))
    mine = jnp.stack(mine)
    swap = [(0, 1), (1, 0)]
    weights, turned = arrange_weights(at, mine, lax.ppermute(mine, "core", swap))

    x_top, x_bottom = edges(x_chunks)
    g_top, g_bottom = edges(g_chunks)
    out_a = conv(3, False, 0, at, x_chunks, x_top, x_bottom, weights)
    grad_a = conv(2, True, 0, at, g_chunks, g_top, g_bottom, turned)
    out_b = conv(3, False, 2, at, x_chunks, x_top, x_bottom, weights)
    grad_b = conv(2, True, 2, at, g_chunks, g_top, g_bottom, turned)
    output_maps = reduce_to_owner(out_a, out_b, "x")
    input_grad = reduce_to_owner(grad_a, grad_b, "y")

    near, far = weight_grads(at, x_chunks, x_top, x_bottom, g_chunks)
    near = near + lax.ppermute(far, "core", swap)
    total = near[0]
    for k, step in ((1, 1), (2, 3), (3, 2)):
        total = total + lax.ppermute(near[k], "z", ring(step))
    cross = [(z * 4 + x, x * 4 + z) for z in range(4) for x in range(4)]
    kernel_grad = lax.ppermute(total, ("z", "x"), cross).reshape(3, 3, 64, LANES)
    return output_maps, input_grad, kernel_grad


def solution(mesh):
    fine = Mesh(mesh.devices.reshape(4, 2, 4, 4), ("z", "core", "x", "y"))
    row, col = ("z", "core"), ("x", "y")
    flat = P(None, row, col)
    taps = P(None, None, col, row)
    return jax.shard_map(
        shards, mesh=fine, in_specs=(flat, taps, flat), out_specs=(flat, flat, taps), check_vma=False
    )
```

```python
import functools

import jax
import jax.numpy as jnp
from jax import lax
from jax.experimental import pallas as pl
from jax.experimental.pallas import tpu as pltpu
from jax.sharding import Mesh, PartitionSpec as P

W = 64
LANES = 128
F32 = jnp.float32
BF16 = jnp.bfloat16
VMEM_LIMIT = 60 * 1024 * 1024

FIRST = [(0, 1), (1, 0), (2, 3), (3, 2)]
SECOND = [(1, 2), (2, 1), (3, 0), (0, 3)]
OPPOSITE = [(i, (i + 2) % 4) for i in range(4)]
SWAP = [(0, 1), (1, 0)]


def params():
    return pltpu.CompilerParams(vmem_limit_bytes=VMEM_LIMIT)


def lane_of(shape):
    return lax.broadcasted_iota(jnp.int32, shape, len(shape) - 1)


def row_of(shape):
    return lax.broadcasted_iota(jnp.int32, shape, len(shape) - 2)


def place_of(member, position):
    odd = lax.rem(position, 2)
    apart = lax.rem(member - position + 4, 4)
    return jnp.where(apart == 0, 0, jnp.where(apart == 2, 3, jnp.where(apart == 1, 1 + odd, 2 - odd)))


def pack_kernel(x_ref, o_ref, rows_ref, mix_ref):
    low = lane_of((32, LANES)) < W
    for side in range(2):
        flat = x_ref[side, 0].astype(F32)
        for p in range(32):
            rows_ref[side, :, p, :] = flat[:, p * LANES : (p + 1) * LANES]
    for h in range(8):
        first = rows_ref[0, h]
        second = rows_ref[1, h]
        mix_ref[h, pl.ds(0, 32, stride=2), :] = jnp.where(low, first, pltpu.roll(second, W, 1))
        mix_ref[h, pl.ds(1, 32, stride=2), :] = jnp.where(low, pltpu.roll(first, W, 1), second)
    for h in range(8):
        o_ref[0, :, h * LANES : (h + 1) * LANES] = mix_ref[h].astype(BF16)


def pack(x):
    return pl.pallas_call(
        pack_kernel,
        out_shape=jax.ShapeDtypeStruct((4, 64, 1024), BF16),
        grid=(4,),
        in_specs=[pl.BlockSpec((2, 1, 8, 4096), lambda q: (0, q, 0, 0))],
        out_specs=pl.BlockSpec((1, 64, 1024), lambda q: (q, 0, 0)),
        scratch_shapes=[pltpu.VMEM((2, 8, 32, LANES), F32), pltpu.VMEM((8, 64, LANES), F32)],
        compiler_params=params(),
        name="pack",
    )(x.reshape(2, 4, 8, 4096))


def finish_kernel(own_a, one_a, two_a, own_b, one_b, two_b, o_ref, mix_ref, rows_ref):
    low = lane_of((32, LANES)) < W
    for half, (own, one, two) in enumerate(((own_a, one_a, two_a), (own_b, one_b, two_b))):

        @pl.when(pl.program_id(0) // 2 == half)
        def _():
            for h in range(8):
                lanes = slice(h * LANES, (h + 1) * LANES)
                mix_ref[h] = own[0, :, lanes] + one[0, 0, :, lanes] + two[0, :, lanes]

    for h in range(8):
        even = mix_ref[h, pl.ds(0, 32, stride=2), :]
        odd = mix_ref[h, pl.ds(1, 32, stride=2), :]
        rows_ref[0, h] = jnp.where(low, even, pltpu.roll(odd, W, 1))
        rows_ref[1, h] = jnp.where(low, pltpu.roll(even, W, 1), odd)
    for side in range(2):
        for p in range(32):
            o_ref[side, 0, :, p * LANES : (p + 1) * LANES] = rows_ref[side, :, p, :].astype(BF16)


def in_half(half):
    return lambda q: jnp.minimum(q, 1) if half == 0 else jnp.maximum(q - 2, 0)


def finish(*pieces):
    specs = []
    for half in range(2):
        at = in_half(half)
        single = pl.BlockSpec((1, 64, 1024), lambda q, at=at: (at(q), 0, 0))
        double = pl.BlockSpec((1, 1, 64, 1024), lambda q, at=at: (0, at(q), 0, 0))
        specs += [single, double, single]
    return pl.pallas_call(
        finish_kernel,
        out_shape=jax.ShapeDtypeStruct((2, 4, 8, 4096), BF16),
        grid=(4,),
        in_specs=specs,
        out_specs=pl.BlockSpec((2, 1, 8, 4096), lambda q: (0, q, 0, 0)),
        scratch_shapes=[pltpu.VMEM((8, 64, LANES), F32), pltpu.VMEM((2, 8, 32, LANES), F32)],
        compiler_params=params(),
        name="finish",
    )(*pieces).reshape(8, 8, 4096)


def weights_kernel(at, mine, other, w_ref, wt_ref, whole):
    z, core, x, y = at[0], at[1], at[2], at[3]
    near = pl.multiple_of(core * LANES, LANES)
    far = pl.multiple_of((1 - core) * LANES, LANES)
    for j in range(4):
        rows = pl.ds(pl.multiple_of(place_of(lax.rem(z + 4 - j, 4), x) * 64, 64), 64)
        for tap in range(9):
            whole[tap, rows, pl.ds(near, LANES)] = mine[j, tap]
            whole[tap, rows, pl.ds(far, LANES)] = other[j, tap]
    listed, channel = row_of((256, 256)), lane_of((256, 256))
    order = jnp.where(
        (place_of(channel // 64, y) == listed // 64) & (channel % 64 == listed % 64), 1.0, 0.0
    ).astype(BF16)
    across = (((1,), (1,)), ((), ()))
    for tap in range(9):
        straight = lax.dot_general(whole[tap], order, across, preferred_element_type=F32).astype(BF16)
        turned = lax.dot_general(order, whole[tap], across, preferred_element_type=F32).astype(BF16)
        a, c = tap // 3, tap % 3
        w_ref[a, :, c * 256 : (c + 1) * 256] = straight
        wt_ref[2 - a, :, (2 - c) * 256 : (3 - c) * 256] = turned


def arrange_weights(at, mine, other):
    shape = jax.ShapeDtypeStruct((3, 256, 768), BF16)
    return pl.pallas_call(
        weights_kernel,
        out_shape=(shape, shape),
        in_specs=[pl.BlockSpec(memory_space=pltpu.SMEM)] + [pl.BlockSpec(memory_space=pltpu.VMEM)] * 2,
        out_specs=[pl.BlockSpec(memory_space=pltpu.VMEM)] * 2,
        scratch_shapes=[pltpu.VMEM((9, 256, 256), BF16)],
        compiler_params=params(),
        name="weights",
    )(at, mine, other)


def lay_shifted(chunks, top, bottom, shifted):
    column = lane_of((64, LANES)) % W
    not_first = jnp.where(column == 0, 0.0, 1.0).astype(BF16)
    not_last = jnp.where(column == W - 1, 0.0, 1.0).astype(BF16)
    for k in range(4):
        rows = k * 64
        for h in range(10):
            if h == 0:
                tile = top[k, 0]
            elif h == 9:
                tile = bottom[k, 0]
            else:
                tile = chunks[k][0, :, (h - 1) * LANES : h * LANES]
            lanes = slice(h * LANES, (h + 1) * LANES)
            shifted[rows : rows + 64, lanes] = pltpu.roll(tile, 1, 1) * not_first
            shifted[256 + rows : 320 + rows, lanes] = tile
            shifted[512 + rows : 576 + rows, lanes] = pltpu.roll(tile, LANES - 1, 1) * not_last


def conv_kernel(at, c0, c1, c2, c3, top, bottom, w_ref, own_a, next_a, send_a, own_b, next_b, send_b, shifted, total):
    lay_shifted((c0, c1, c2, c3), top, bottom, shifted)
    for n in range(4):
        part = None
        for a in range(3):
            start = a * LANES + n * 256
            term = jnp.dot(w_ref[a], shifted[:, start : start + 256], preferred_element_type=F32)
            part = term if part is None else part + term
        total[:, n * 256 : (n + 1) * 256] = part

    @pl.when(pl.program_id(0) < 2)
    def _():
        own_a[0] = total[0:64]
        send_a[0, 0] = total[64:128]
        next_a[0] = total[128:192]
        send_a[1, 0] = total[192:256]

    @pl.when(pl.program_id(0) >= 2)
    def _():
        own_b[0] = total[0:64]
        next_b[0] = total[64:128]
        send_b[0, 0] = total[128:192]
        send_b[1, 0] = total[192:256]


def conv(name, at, chunks, top, bottom, weights):
    single = jax.ShapeDtypeStruct((2, 64, 1024), F32)
    double = jax.ShapeDtypeStruct((2, 2, 64, 1024), F32)
    chunk = pl.BlockSpec((1, 64, 1024), lambda q: (q, 0, 0))
    edge = pl.BlockSpec((4, 1, 64, LANES), lambda q: (0, q, 0, 0))
    specs = []
    for half in range(2):
        where = in_half(half)
        one = pl.BlockSpec((1, 64, 1024), lambda q, where=where: (where(q), 0, 0))
        two = pl.BlockSpec((2, 1, 64, 1024), lambda q, where=where: (0, where(q), 0, 0))
        specs += [one, one, two]
    return pl.pallas_call(
        conv_kernel,
        out_shape=(single, single, double) * 2,
        grid=(4,),
        in_specs=[pl.BlockSpec(memory_space=pltpu.SMEM)]
        + [chunk] * 4
        + [edge] * 2
        + [pl.BlockSpec((3, 256, 768), lambda q: (0, 0, 0))],
        out_specs=specs,
        scratch_shapes=[pltpu.VMEM((768, 1280), BF16), pltpu.VMEM((256, 1024), F32)],
        compiler_params=params(),
        cost_estimate=pl.CostEstimate(flops=4831838208, bytes_accessed=12000000, transcendentals=0),
        name=name,
    )(at, *chunks, top, bottom, weights)


def kernel_grad_kernel(at, x0, x1, x2, x3, top, bottom, g0, g1, g2, g3, mine, other, shifted, grads, total):
    z, core, x, y = at[0], at[1], at[2], at[3]
    q = pl.program_id(0)
    lay_shifted((x0, x1, x2, x3), top, bottom, shifted)
    for k, g_ref in enumerate((g0, g1, g2, g3)):
        grads[k * 64 : (k + 1) * 64, :] = g_ref[0]

    @pl.when(q == 0)
    def _():
        total[...] = jnp.zeros_like(total)

    for a in range(3):
        total[a] += lax.dot_general(
            grads[...],
            shifted[:, a * LANES : a * LANES + 1024],
            (((1,), (1,)), ((), ())),
            preferred_element_type=F32,
        )

    @pl.when(q == 3)
    def _():
        for half, o_ref in ((core, mine), (1 - core, other)):
            second = jnp.where(half == y // 2, 0, 1)
            straight = second == lax.rem(y, 2)
            for k in range(4):
                member = lax.rem(z + (0, 1, 3, 2)[k], 4)
                rows = pl.ds(pl.multiple_of(place_of(member, x) * 64, 64), 64)
                for a in range(3):
                    for c in range(3):
                        lanes = pl.ds(pl.multiple_of(c * 256 + second * LANES, LANES), LANES)
                        tile = total[a, rows, lanes]
                        o_ref[k, a * 3 + c] = jnp.where(straight, tile, pltpu.roll(tile, W, 1))


def weight_grads(at, chunks, top, bottom, grads):
    shape = jax.ShapeDtypeStruct((4, 9, 64, LANES), F32)
    chunk = pl.BlockSpec((1, 64, 1024), lambda q: (q, 0, 0))
    edge = pl.BlockSpec((4, 1, 64, LANES), lambda q: (0, q, 0, 0))
    whole = pl.BlockSpec((4, 9, 64, LANES), lambda q: (0, 0, 0, 0))
    return pl.pallas_call(
        kernel_grad_kernel,
        out_shape=(shape,) * 2,
        grid=(4,),
        in_specs=[pl.BlockSpec(memory_space=pltpu.SMEM)] + [chunk] * 4 + [edge] * 2 + [chunk] * 4,
        out_specs=[whole] * 2,
        scratch_shapes=[
            pltpu.VMEM((768, 1280), BF16),
            pltpu.VMEM((256, 1024), BF16),
            pltpu.VMEM((3, 256, 768), F32),
        ],
        compiler_params=params(),
        cost_estimate=pl.CostEstimate(flops=4831838208, bytes_accessed=9000000, transcendentals=0),
        name="weight_grads",
    )(at, *chunks, top, bottom, *grads)


def ring(step):
    return [(i, (i + step) % 4) for i in range(4)]


def after(value, *others):
    return lax.optimization_barrier((value, *others))[0]


def gather(block, axis):
    return (
        block,
        lax.ppermute(block, axis, FIRST),
        lax.ppermute(block, axis, SECOND),
        lax.ppermute(block, axis, OPPOSITE),
    )


def edges(chunks):
    forward = [(i, i + 1) for i in range(7)]
    backward = [(j, i) for i, j in forward]
    last = jnp.stack([chunk[:, :, -LANES:] for chunk in chunks])
    first = jnp.stack([chunk[:, :, :LANES] for chunk in chunks])
    return lax.ppermute(last, ("z", "core"), forward), lax.ppermute(first, ("z", "core"), backward)


def reduce_first(parts, axis):
    return lax.ppermute(parts[2], axis, FIRST), lax.ppermute(parts[5], axis, SECOND)


def reduce_second(parts, arrived, axis):
    one_a, one_b = arrived
    two_a = lax.ppermute(parts[1] + one_a[1], axis, SECOND)
    two_b = lax.ppermute(parts[4] + one_b[1], axis, FIRST)
    return finish(parts[0], one_a, two_a, parts[3], one_b, two_b)


def shards(images, kernel, upstream):
    at = jnp.stack([lax.axis_index(n) for n in ("z", "core", "x", "y")]).astype(jnp.int32)
    x_chunks = gather(pack(images), "y")

    block = kernel.reshape(9, 64, LANES)
    mine = []
    for j in range(4):
        pairs = [(z * 4 + x, ((x + j) % 4) * 4 + z) for z in range(4) for x in range(4)]
        mine.append(lax.ppermute(block, ("z", "x"), pairs))
    mine = jnp.stack(mine)
    g_chunks = gather(pack(upstream), "x")
    weights, turned = arrange_weights(at, mine, lax.ppermute(mine, "core", SWAP))

    x_top, x_bottom = edges(x_chunks)
    out = conv("conv_out", at, x_chunks, x_top, x_bottom, weights)
    g_top, g_bottom = edges(g_chunks)
    grad = conv("conv_grad", after(at, out[0]), g_chunks, g_top, g_bottom, turned)
    out_one = reduce_first(out, "x")
    grad_one = reduce_first(grad, "y")

    near, far = weight_grads(after(at, grad[0]), x_chunks, x_top, x_bottom, g_chunks)
    near = near + lax.ppermute(far, "core", SWAP)
    output_maps = reduce_second(out, out_one, "x")
    input_grad = reduce_second(grad, grad_one, "y")
    total = near[0]
    for k, step in ((1, 1), (2, 3), (3, 2)):
        total = total + lax.ppermute(near[k], "z", ring(step))
    cross = [(z * 4 + x, x * 4 + z) for z in range(4) for x in range(4)]
    kernel_grad = lax.ppermute(total, ("z", "x"), cross).reshape(3, 3, 64, LANES)
    return output_maps, input_grad, kernel_grad


def solution(mesh):
    fine = Mesh(mesh.devices.reshape(4, 2, 4, 4), ("z", "core", "x", "y"))
    row, col = ("z", "core"), ("x", "y")
    flat = P(None, row, col)
    taps = P(None, None, col, row)
    return jax.shard_map(
        shards, mesh=fine, in_specs=(flat, taps, flat), out_specs=(flat, flat, taps), check_vma=False
    )
```

```python
import functools

import jax
import jax.numpy as jnp
from jax import lax
from jax.experimental import pallas as pl
from jax.experimental.pallas import tpu as pltpu
from jax.sharding import Mesh, PartitionSpec as P


W = 64
LANES = 128
F32 = jnp.float32
BF16 = jnp.bfloat16
VMEM_LIMIT = 60 * 1024 * 1024

FIRST = [(0, 1), (1, 0), (2, 3), (3, 2)]
SECOND = [(1, 2), (2, 1), (3, 0), (0, 3)]
OPPOSITE = [(i, (i + 2) % 4) for i in range(4)]
SWAP = [(0, 1), (1, 0)]


def params():
    return pltpu.CompilerParams(vmem_limit_bytes=VMEM_LIMIT)


def lane_of(shape):
    return lax.broadcasted_iota(jnp.int32, shape, len(shape) - 1)


def row_of(shape):
    return lax.broadcasted_iota(jnp.int32, shape, len(shape) - 2)


def place_of(member, position):
    odd = lax.rem(position, 2)
    apart = lax.rem(member - position + 4, 4)
    return jnp.where(apart == 0, 0, jnp.where(apart == 2, 3, jnp.where(apart == 1, 1 + odd, 2 - odd)))


def pack_kernel(x_ref, o_ref, rows_ref, mix_ref):
    low = lane_of((32, LANES)) < W
    for q in range(4):
        for side in range(2):
            flat = x_ref[q + 4 * side].astype(F32)
            for p in range(32):
                rows_ref[side, :, p, :] = flat[:, p * LANES : (p + 1) * LANES]
        for h in range(8):
            first = rows_ref[0, h]
            second = rows_ref[1, h]
            mix_ref[h, pl.ds(0, 32, stride=2), :] = jnp.where(low, first, pltpu.roll(second, W, 1))
            mix_ref[h, pl.ds(1, 32, stride=2), :] = jnp.where(low, pltpu.roll(first, W, 1), second)
        for h in range(8):
            o_ref[q, :, h * LANES : (h + 1) * LANES] = mix_ref[h].astype(BF16)


def pack(x):
    return pl.pallas_call(
        pack_kernel,
        out_shape=jax.ShapeDtypeStruct((4, 64, 1024), BF16),
        in_specs=[pl.BlockSpec(memory_space=pltpu.VMEM)],
        out_specs=pl.BlockSpec(memory_space=pltpu.VMEM),
        scratch_shapes=[pltpu.VMEM((2, 8, 32, LANES), F32), pltpu.VMEM((8, 64, LANES), F32)],
        compiler_params=params(),
        name="pack",
    )(x)


ROWS = ((1, 2, 3, 4), (5, 6, 7, 0))


def finish_kernel(own_a, one_a, two_a, own_b, one_b, two_b, o_ref, mix_ref, rows_ref):
    low = lane_of((32, LANES)) < W
    for q in range(4):
        for rows, (own, one, two) in zip(ROWS, ((own_a, one_a, two_a), (own_b, one_b, two_b))):
            for j, h in enumerate(rows):
                lanes = slice(j * LANES, (j + 1) * LANES)
                mix_ref[h] = own[q, :, lanes] + one[0, q, :, lanes] + two[q, :, lanes]
        for h in range(8):
            even = mix_ref[h, pl.ds(0, 32, stride=2), :]
            odd = mix_ref[h, pl.ds(1, 32, stride=2), :]
            rows_ref[0, h] = jnp.where(low, even, pltpu.roll(odd, W, 1))
            rows_ref[1, h] = jnp.where(low, pltpu.roll(even, W, 1), odd)
        for side in range(2):
            for p in range(32):
                o_ref[q + 4 * side, :, p * LANES : (p + 1) * LANES] = rows_ref[side, :, p, :].astype(BF16)


def finish(*pieces):
    single = pl.BlockSpec((4, 64, 512), lambda i: (0, 0, 0))
    double = pl.BlockSpec((1, 4, 64, 512), lambda i: (0, 0, 0, 0))
    return pl.pallas_call(
        finish_kernel,
        out_shape=jax.ShapeDtypeStruct((8, 8, 4096), BF16),
        grid=(1,),
        in_specs=[single, double, single] * 2,
        out_specs=pl.BlockSpec((8, 8, 4096), lambda i: (0, 0, 0)),
        scratch_shapes=[pltpu.VMEM((8, 64, LANES), F32), pltpu.VMEM((2, 8, 32, LANES), F32)],
        compiler_params=params(),
        name="finish",
    )(*pieces)


def weights_kernel(at, mine, other, w_ref, wt_ref, whole):
    z, core, x, y = at[0], at[1], at[2], at[3]
    for ref, side in ((mine, core), (other, 1 - core)):
        for k in range(2):
            member = lax.rem(z + 8 - 2 * k - side, 4)
            rows = pl.ds(pl.multiple_of(place_of(member, x) * 64, 64), 64)
            for tap in range(9):
                for which, half in ((0, side), (1, 1 - side)):
                    lanes = pl.ds(pl.multiple_of(half * LANES, LANES), LANES)
                    whole[tap, rows, lanes] = ref[k, which, tap]
    listed, channel = row_of((256, 256)), lane_of((256, 256))
    order = jnp.where(
        (place_of(channel // 64, y) == listed // 64) & (channel % 64 == listed % 64), 1.0, 0.0
    ).astype(BF16)
    across = (((1,), (1,)), ((), ()))
    for tap in range(9):
        straight = lax.dot_general(whole[tap], order, across, preferred_element_type=F32).astype(BF16)
        turned = lax.dot_general(order, whole[tap], across, preferred_element_type=F32).astype(BF16)
        a, c = tap // 3, tap % 3
        w_ref[a, :, c * 256 : (c + 1) * 256] = straight
        wt_ref[2 - a, :, (2 - c) * 256 : (3 - c) * 256] = turned


def arrange_weights(at, mine, other):
    shape = jax.ShapeDtypeStruct((3, 256, 768), BF16)
    return pl.pallas_call(
        weights_kernel,
        out_shape=(shape, shape),
        in_specs=[pl.BlockSpec(memory_space=pltpu.SMEM)] + [pl.BlockSpec(memory_space=pltpu.VMEM)] * 2,
        out_specs=[pl.BlockSpec(memory_space=pltpu.VMEM)] * 2,
        scratch_shapes=[pltpu.VMEM((9, 256, 256), BF16)],
        compiler_params=params(),
        name="weights",
    )(at, mine, other)


def lay_shifted(chunks, top, bottom, rows, shifted):
    column = lane_of((64, LANES)) % W
    not_first = jnp.where(column == 0, 0.0, 1.0).astype(BF16)
    not_last = jnp.where(column == W - 1, 0.0, 1.0).astype(BF16)
    for k in range(4):
        at = k * 64
        for j, h in enumerate(rows):
            if h == -1:
                tile = top[k, 0]
            elif h == 8:
                tile = bottom[k, 0]
            else:
                tile = chunks[k][0, :, h * LANES : (h + 1) * LANES]
            lanes = slice(j * LANES, (j + 1) * LANES)
            shifted[at : at + 64, lanes] = pltpu.roll(tile, 1, 1) * not_first
            shifted[256 + at : 320 + at, lanes] = tile
            shifted[512 + at : 576 + at, lanes] = pltpu.roll(tile, LANES - 1, 1) * not_last


def conv_kernel(half, at, c0, c1, c2, c3, *refs):
    top, bottom = refs[:2] if half else (None, None)
    w_ref, own, following, send, shifted = refs[2 * half :]
    rows = (4, 5, 6, 7, 8, -1, 0, 1) if half else (0, 1, 2, 3, 4, 5)
    lay_shifted((c0, c1, c2, c3), top, bottom, rows, shifted)
    for n in range(2):
        part = None
        for a in range(3):
            first = 2 * n + a
            second = 5 + a if half and n else first + 1
            source = jnp.concatenate(
                [shifted[:, i * LANES : (i + 1) * LANES] for i in (first, second)], axis=1
            )
            term = jnp.dot(w_ref[a], source, preferred_element_type=F32)
            part = term if part is None else part + term
        lanes = slice(n * 256, (n + 1) * 256)
        own[0, :, lanes] = part[0:64]
        first_out, second_out = (following.at[0], send.at[0, 0]) if half else (send.at[0, 0], following.at[0])
        first_out[:, lanes] = part[64:128]
        second_out[:, lanes] = part[128:192]
        send[1, 0, :, lanes] = part[192:256]


def conv(half, at, chunks, sides, weights):
    single = jax.ShapeDtypeStruct((4, 64, 512), F32)
    double = jax.ShapeDtypeStruct((2, 4, 64, 512), F32)
    chunk = pl.BlockSpec((1, 64, 1024), lambda q: (q, 0, 0))
    edge = pl.BlockSpec((4, 1, 64, LANES), lambda q: (0, q, 0, 0))
    one = pl.BlockSpec((1, 64, 512), lambda q: (q, 0, 0))
    two = pl.BlockSpec((2, 1, 64, 512), lambda q: (0, q, 0, 0))
    sides = sides if half else ()
    return pl.pallas_call(
        functools.partial(conv_kernel, half),
        out_shape=(single, single, double),
        grid=(4,),
        in_specs=[pl.BlockSpec(memory_space=pltpu.SMEM)]
        + [chunk] * 4
        + [edge] * len(sides)
        + [pl.BlockSpec((3, 256, 768), lambda q: (0, 0, 0))],
        out_specs=[one, one, two],
        scratch_shapes=[pltpu.VMEM((768, 1024 if half else 768), BF16)],
        compiler_params=params(),
        cost_estimate=pl.CostEstimate(flops=2415919104, bytes_accessed=6000000, transcendentals=0),
    )(at, *chunks, *sides, weights)


def kernel_grad_kernel(at, x0, x1, x2, x3, top, bottom, g0, g1, g2, g3, mine, other, shifted, grads, total):
    z, core, x, y = at[0], at[1], at[2], at[3]
    q = pl.program_id(0)
    lay_shifted((x0, x1, x2, x3), top, bottom, range(-1, 9), shifted)
    for k, g_ref in enumerate((g0, g1, g2, g3)):
        grads[k * 64 : (k + 1) * 64, :] = g_ref[0]

    @pl.when(q == 0)
    def _():
        total[...] = jnp.zeros_like(total)

    for a in range(3):
        total[a] += lax.dot_general(
            grads[...],
            shifted[:, a * LANES : a * LANES + 1024],
            (((1,), (1,)), ((), ())),
            preferred_element_type=F32,
        )

    @pl.when(q == 3)
    def _():
        for half, o_ref in ((core, mine), (1 - core, other)):
            second = jnp.where(half == y // 2, 0, 1)
            straight = second == lax.rem(y, 2)
            for k in range(4):
                member = lax.rem(z + (0, 1, 3, 2)[k], 4)
                rows = pl.ds(pl.multiple_of(place_of(member, x) * 64, 64), 64)
                for a in range(3):
                    for c in range(3):
                        lanes = pl.ds(pl.multiple_of(c * 256 + second * LANES, LANES), LANES)
                        tile = total[a, rows, lanes]
                        o_ref[k, a * 3 + c] = jnp.where(straight, tile, pltpu.roll(tile, W, 1))


def weight_grads(at, chunks, top, bottom, grads):
    shape = jax.ShapeDtypeStruct((4, 9, 64, LANES), F32)
    chunk = pl.BlockSpec((1, 64, 1024), lambda q: (q, 0, 0))
    edge = pl.BlockSpec((4, 1, 64, LANES), lambda q: (0, q, 0, 0))
    whole = pl.BlockSpec((4, 9, 64, LANES), lambda q: (0, 0, 0, 0))
    return pl.pallas_call(
        kernel_grad_kernel,
        out_shape=(shape,) * 2,
        grid=(4,),
        in_specs=[pl.BlockSpec(memory_space=pltpu.SMEM)] + [chunk] * 4 + [edge] * 2 + [chunk] * 4,
        out_specs=[whole] * 2,
        scratch_shapes=[
            pltpu.VMEM((768, 1280), BF16),
            pltpu.VMEM((256, 1024), BF16),
            pltpu.VMEM((3, 256, 768), F32),
        ],
        compiler_params=params(),
        cost_estimate=pl.CostEstimate(flops=4831838208, bytes_accessed=9000000, transcendentals=0),
        name="weight_grads",
    )(at, *chunks, top, bottom, *grads)


def ring(step):
    return [(i, (i + step) % 4) for i in range(4)]


def after(value, *others):
    return lax.optimization_barrier((value, *others))[0]


def gather(block, axis):
    return (
        block, lax.ppermute(block, axis, FIRST), lax.ppermute(block, axis, SECOND), lax.ppermute(block, axis, OPPOSITE)
    )


def edges(chunks):
    forward = [(i, i + 1) for i in range(7)]
    backward = [(j, i) for i, j in forward]
    last = jnp.stack([chunk[:, :, -LANES:] for chunk in chunks])
    first = jnp.stack([chunk[:, :, :LANES] for chunk in chunks])
    return (lax.ppermute(last, ("z", "core"), forward), lax.ppermute(first, ("z", "core"), backward))


def reduce_second(a, b, one_a, one_b, axis):
    two_a = lax.ppermute(a[1] + one_a[1], axis, SECOND)
    two_b = lax.ppermute(b[1] + one_b[1], axis, FIRST)
    return finish(a[0], one_a, two_a, b[0], one_b, two_b)


def fetch_weights(at, block):
    both = jnp.stack([block, lax.ppermute(block, "core", SWAP)])
    got = []
    for k in range(2):
        pairs = [
            ((z * 2 + s) * 4 + x, (((x + 2 * k + s) % 4) * 2 + s) * 4 + z)
            for z in range(4)
            for s in range(2)
            for x in range(4)
        ]
        got.append(lax.ppermute(both, ("z", "core", "x"), pairs))
    got = jnp.stack(got)
    return arrange_weights(at, got, lax.ppermute(got, "core", SWAP))


def step(images, kernel, upstream):
    at = jnp.stack([lax.axis_index(n) for n in ("z", "core", "x", "y")]).astype(jnp.int32)
    weights, turned = fetch_weights(at, kernel.reshape(9, 64, LANES))
    x = pack(images)
    x_chunks = gather(x, "y")
    g = pack(upstream)
    g_chunks = gather(g, "x")

    x_sides = edges(x_chunks)
    g_sides = edges(g_chunks)
    out_a = conv(0, at, x_chunks, x_sides, weights)
    out_one_a = lax.ppermute(out_a[2], "x", FIRST)
    out_b = conv(1, after(at, out_a[0]), x_chunks, x_sides, weights)
    out_one_b = lax.ppermute(out_b[2], "x", SECOND)
    grad_a = conv(0, after(at, out_b[0]), g_chunks, g_sides, turned)
    grad_one_a = lax.ppermute(grad_a[2], "y", FIRST)
    grad_b = conv(1, after(at, grad_a[0]), g_chunks, g_sides, turned)
    grad_one_b = lax.ppermute(grad_b[2], "y", SECOND)

    near, far = weight_grads(after(at, grad_b[0]), x_chunks, *x_sides, g_chunks)
    near = near + lax.ppermute(far, "core", SWAP)
    output_maps = reduce_second(out_a, out_b, out_one_a, out_one_b, "x")
    input_grad = reduce_second(grad_a, grad_b, grad_one_a, grad_one_b, "y")
    total = near[0]
    for k, turn in ((1, 1), (2, 3), (3, 2)):
        total = total + lax.ppermute(near[k], "z", ring(turn))
    cross = [(z * 4 + x, x * 4 + z) for z in range(4) for x in range(4)]
    kernel_grad = lax.ppermute(total, ("z", "x"), cross).reshape(3, 3, 64, LANES)
    return output_maps, input_grad, kernel_grad


def solution(mesh):
    fine = Mesh(mesh.devices.reshape(4, 2, 4, 4), ("z", "core", "x", "y"))
    row, col = ("z", "core"), ("x", "y")
    flat = P(None, row, col)
    taps = P(None, None, col, row)
    return jax.shard_map(step, mesh=fine, in_specs=(flat, taps, flat), out_specs=(flat, flat, taps), check_vma=False)
```

```python
import functools

import jax
import jax.numpy as jnp
from jax import lax
from jax.experimental import pallas as pl
from jax.experimental.pallas import tpu as pltpu
from jax.sharding import Mesh, PartitionSpec as P


W = 64
LANES = 128
F32 = jnp.float32
BF16 = jnp.bfloat16

FIRST = [(0, 1), (1, 0), (2, 3), (3, 2)]
SECOND = [(1, 2), (2, 1), (3, 0), (0, 3)]
OPPOSITE = [(i, (i + 2) % 4) for i in range(4)]
SWAP = [(0, 1), (1, 0)]


def params(mib):
    return pltpu.CompilerParams(vmem_limit_bytes=mib * 1024 * 1024)


def lane_of(shape):
    return lax.broadcasted_iota(jnp.int32, shape, len(shape) - 1)


def row_of(shape):
    return lax.broadcasted_iota(jnp.int32, shape, len(shape) - 2)


def place_of(member, position):
    odd = lax.rem(position, 2)
    apart = lax.rem(member - position + 4, 4)
    return jnp.where(apart == 0, 0, jnp.where(apart == 2, 3, jnp.where(apart == 1, 1 + odd, 2 - odd)))


def pack_kernel(x_hbm, g_hbm, x_out, g_out, taken, given, rows_ref, mix_ref, in_sem, out_sem):
    low = lane_of((32, LANES)) < W
    pieces = [(t, q) for t in range(2) for q in range(4)]
    ins, outs = (x_hbm, g_hbm), (x_out, g_out)

    def fetch(t, q, side):
        return pltpu.make_async_copy(ins[t].at[q + 4 * side], taken.at[t, q, side], in_sem.at[t, q, side])

    def put(t, q):
        return pltpu.make_async_copy(given.at[t, q], outs[t].at[q], out_sem.at[t, q])

    for t, q in pieces:
        for side in range(2):
            fetch(t, q, side).start()
    for t, q in pieces:
        b = q % 2
        for side in range(2):
            fetch(t, q, side).wait()
            flat = taken[t, q, side].astype(F32)
            for p in range(32):
                rows_ref[b, side, :, p, :] = flat[:, p * LANES : (p + 1) * LANES]
        for h in range(8):
            first = rows_ref[b, 0, h]
            second = rows_ref[b, 1, h]
            mix_ref[b, h, pl.ds(0, 32, stride=2), :] = jnp.where(low, first, pltpu.roll(second, W, 1))
            mix_ref[b, h, pl.ds(1, 32, stride=2), :] = jnp.where(low, pltpu.roll(first, W, 1), second)
        for h in range(8):
            given[t, q, :, h * LANES : (h + 1) * LANES] = mix_ref[b, h].astype(BF16)
        put(t, q).start()
    for t, q in pieces:
        put(t, q).wait()


def pack(x, g):
    shape = jax.ShapeDtypeStruct((4, 64, 1024), BF16)
    anywhere = pl.BlockSpec(memory_space=pl.ANY)
    return pl.pallas_call(
        pack_kernel,
        out_shape=(shape, shape),
        in_specs=[pl.BlockSpec(memory_space=pltpu.HBM)] * 2,
        out_specs=[anywhere] * 2,
        scratch_shapes=[
            pltpu.VMEM((2, 4, 2, 8, 4096), BF16),
            pltpu.VMEM((2, 4, 64, 1024), BF16),
            pltpu.VMEM((2, 2, 8, 32, LANES), F32),
            pltpu.VMEM((2, 8, 64, LANES), F32),
            pltpu.SemaphoreType.DMA((2, 4, 2)),
            pltpu.SemaphoreType.DMA((2, 4)),
        ],
        compiler_params=params(8),
        name="pack",
    )(x, g)


ROWS = ((1, 2, 3, 4), (5, 6, 7, 0))


def finish_kernel(own_a, one_a, two_a, own_b, one_b, two_b, o_hbm, taken, given, mix_ref, rows_ref, in_sem, out_sem):
    low = lane_of((32, LANES)) < W
    pieces = ((own_a, one_a, two_a), (own_b, one_b, two_b))

    def fetch(q, half, i):
        ref = pieces[half][i]
        source = ref.at[0, q] if i == 1 else ref.at[q]
        return pltpu.make_async_copy(source, taken.at[q, half, i], in_sem.at[q, half, i])

    def put(q, side):
        return pltpu.make_async_copy(given.at[q, side], o_hbm.at[q + 4 * side], out_sem.at[q, side])

    parts = [(half, i) for half in range(2) for i in range(3)]
    for q in range(4):
        for half, i in parts:
            fetch(q, half, i).start()
    for q in range(4):
        b = q % 2
        for half, i in parts:
            fetch(q, half, i).wait()
        for half, rows in enumerate(ROWS):
            for j, h in enumerate(rows):
                lanes = slice(j * LANES, (j + 1) * LANES)
                mix_ref[b, h] = taken[q, half, 0, :, lanes] + taken[q, half, 1, :, lanes] + taken[q, half, 2, :, lanes]
        for h in range(8):
            even = mix_ref[b, h, pl.ds(0, 32, stride=2), :]
            odd = mix_ref[b, h, pl.ds(1, 32, stride=2), :]
            rows_ref[b, 0, h] = jnp.where(low, even, pltpu.roll(odd, W, 1))
            rows_ref[b, 1, h] = jnp.where(low, pltpu.roll(even, W, 1), odd)
        for side in range(2):
            for p in range(32):
                given[q, side, :, p * LANES : (p + 1) * LANES] = rows_ref[b, side, :, p, :].astype(BF16)
            put(q, side).start()
    for q in range(4):
        for side in range(2):
            put(q, side).wait()


def finish(*pieces):
    anywhere = pl.BlockSpec(memory_space=pl.ANY)
    return pl.pallas_call(
        finish_kernel,
        out_shape=jax.ShapeDtypeStruct((8, 8, 4096), BF16),
        in_specs=[anywhere] * 6,
        out_specs=anywhere,
        scratch_shapes=[
            pltpu.VMEM((4, 2, 3, 64, 512), F32),
            pltpu.VMEM((4, 2, 8, 4096), BF16),
            pltpu.VMEM((2, 8, 64, LANES), F32),
            pltpu.VMEM((2, 2, 8, 32, LANES), F32),
            pltpu.SemaphoreType.DMA((4, 2, 3)),
            pltpu.SemaphoreType.DMA((4, 2)),
        ],
        compiler_params=params(8),
        name="finish",
    )(*pieces)


def weights_kernel(at, mine, other, w_ref, wt_ref, whole):
    z, core, x, y = at[0], at[1], at[2], at[3]
    for ref, side in ((mine, core), (other, 1 - core)):
        for k in range(2):
            member = lax.rem(z + 8 - 2 * k - side, 4)
            rows = pl.ds(pl.multiple_of(place_of(member, x) * 64, 64), 64)
            for tap in range(9):
                for which, half in ((0, side), (1, 1 - side)):
                    lanes = pl.ds(pl.multiple_of(half * LANES, LANES), LANES)
                    whole[tap, rows, lanes] = ref[k, which, tap]
    listed, channel = row_of((256, 256)), lane_of((256, 256))
    order = jnp.where(
        (place_of(channel // 64, y) == listed // 64) & (channel % 64 == listed % 64), 1.0, 0.0
    ).astype(BF16)
    across = (((1,), (1,)), ((), ()))
    for tap in range(9):
        straight = lax.dot_general(whole[tap], order, across, preferred_element_type=F32).astype(BF16)
        turned = lax.dot_general(order, whole[tap], across, preferred_element_type=F32).astype(BF16)
        a, c = tap // 3, tap % 3
        w_ref[a, :, c * 256 : (c + 1) * 256] = straight
        wt_ref[2 - a, :, (2 - c) * 256 : (3 - c) * 256] = turned


def arrange_weights(at, mine, other):
    shape = jax.ShapeDtypeStruct((3, 256, 768), BF16)
    return pl.pallas_call(
        weights_kernel,
        out_shape=(shape, shape),
        in_specs=[pl.BlockSpec(memory_space=pltpu.SMEM)] + [pl.BlockSpec(memory_space=pltpu.VMEM)] * 2,
        out_specs=[pl.BlockSpec(memory_space=pltpu.VMEM)] * 2,
        scratch_shapes=[pltpu.VMEM((9, 256, 256), BF16)],
        compiler_params=params(20),
        name="weights",
    )(at, mine, other)


def lay_shifted(chunks, top, bottom, rows, shifted):
    column = lane_of((64, LANES)) % W
    not_first = jnp.where(column == 0, 0.0, 1.0).astype(BF16)
    not_last = jnp.where(column == W - 1, 0.0, 1.0).astype(BF16)
    for k in range(4):
        at = k * 64
        for j, h in enumerate(rows):
            if h == -1:
                tile = top[k, 0]
            elif h == 8:
                tile = bottom[k, 0]
            else:
                tile = chunks[k][0, :, h * LANES : (h + 1) * LANES]
            lanes = slice(j * LANES, (j + 1) * LANES)
            shifted[at : at + 64, lanes] = pltpu.roll(tile, 1, 1) * not_first
            shifted[256 + at : 320 + at, lanes] = tile
            shifted[512 + at : 576 + at, lanes] = pltpu.roll(tile, LANES - 1, 1) * not_last


def conv_kernel(halves, rows, at, c0, c1, c2, c3, *refs):
    edged = 1 in halves
    top, bottom = refs[:2] if edged else (None, None)
    refs = refs[2 * edged :]
    w_ref, shifted = refs[0], refs[-1]
    lay_shifted((c0, c1, c2, c3), top, bottom, rows, shifted)
    for i, half in enumerate(halves):
        own, following, send = refs[1 + 3 * i : 4 + 3 * i]
        for n in range(2):
            part = None
            for a in range(3):
                places = [rows.index(h - 1 + a) for h in ROWS[half][2 * n : 2 * n + 2]]
                source = jnp.concatenate([shifted[:, j * LANES : (j + 1) * LANES] for j in places], axis=1)
                term = jnp.dot(w_ref[a], source, preferred_element_type=F32)
                part = term if part is None else part + term
            lanes = slice(n * 256, (n + 1) * 256)
            own[0, :, lanes] = part[0:64]
            pair = (following.at[0], send.at[0, 0]) if half else (send.at[0, 0], following.at[0])
            pair[0][:, lanes] = part[64:128]
            pair[1][:, lanes] = part[128:192]
            send[1, 0, :, lanes] = part[192:256]


def conv(halves, at, chunks, sides, weights):
    rows = {(0,): (0, 1, 2, 3, 4, 5), (1,): (4, 5, 6, 7, 8, -1, 0, 1)}.get(halves, tuple(range(-1, 9)))
    single = jax.ShapeDtypeStruct((4, 64, 512), F32)
    double = jax.ShapeDtypeStruct((2, 4, 64, 512), F32)
    chunk = pl.BlockSpec((1, 64, 1024), lambda q: (q, 0, 0))
    edge = pl.BlockSpec((4, 1, 64, LANES), lambda q: (0, q, 0, 0))
    one = pl.BlockSpec((1, 64, 512), lambda q: (q, 0, 0))
    two = pl.BlockSpec((2, 1, 64, 512), lambda q: (0, q, 0, 0))
    sides = sides if 1 in halves else ()
    return pl.pallas_call(
        functools.partial(conv_kernel, halves, rows),
        out_shape=(single, single, double) * len(halves),
        grid=(4,),
        in_specs=[pl.BlockSpec(memory_space=pltpu.SMEM)]
        + [chunk] * 4
        + [edge] * len(sides)
        + [pl.BlockSpec((3, 256, 768), lambda q: (0, 0, 0))],
        out_specs=[one, one, two] * len(halves),
        scratch_shapes=[pltpu.VMEM((768, len(rows) * LANES), BF16)],
        compiler_params=params(16),
        cost_estimate=pl.CostEstimate(
            flops=2415919104 * len(halves), bytes_accessed=6000000 * len(halves), transcendentals=0
        ),
    )(at, *chunks, *sides, weights)


def kernel_grad_kernel(at, x0, x1, x2, x3, top, bottom, g0, g1, g2, g3, mine, other, shifted, grads, total):
    z, core, x, y = at[0], at[1], at[2], at[3]
    q = pl.program_id(0)
    lay_shifted((x0, x1, x2, x3), top, bottom, range(-1, 9), shifted)
    for k, g_ref in enumerate((g0, g1, g2, g3)):
        grads[k * 64 : (k + 1) * 64, :] = g_ref[0]

    @pl.when(q == 0)
    def _():
        total[...] = jnp.zeros_like(total)

    for a in range(3):
        total[a] += lax.dot_general(
            grads[...],
            shifted[:, a * LANES : a * LANES + 1024],
            (((1,), (1,)), ((), ())),
            preferred_element_type=F32,
        )

    @pl.when(q == 3)
    def _():
        for half, o_ref in ((core, mine), (1 - core, other)):
            second = jnp.where(half == y // 2, 0, 1)
            straight = second == lax.rem(y, 2)
            for k in range(4):
                member = lax.rem(z + (0, 1, 3, 2)[k], 4)
                rows = pl.ds(pl.multiple_of(place_of(member, x) * 64, 64), 64)
                for a in range(3):
                    for c in range(3):
                        lanes = pl.ds(pl.multiple_of(c * 256 + second * LANES, LANES), LANES)
                        tile = total[a, rows, lanes]
                        o_ref[k, a * 3 + c] = jnp.where(straight, tile, pltpu.roll(tile, W, 1))


def weight_grads(at, chunks, top, bottom, grads):
    shape = jax.ShapeDtypeStruct((4, 9, 64, LANES), F32)
    chunk = pl.BlockSpec((1, 64, 1024), lambda q: (q, 0, 0))
    edge = pl.BlockSpec((4, 1, 64, LANES), lambda q: (0, q, 0, 0))
    whole = pl.BlockSpec((4, 9, 64, LANES), lambda q: (0, 0, 0, 0))
    return pl.pallas_call(
        kernel_grad_kernel,
        out_shape=(shape,) * 2,
        grid=(4,),
        in_specs=[pl.BlockSpec(memory_space=pltpu.SMEM)] + [chunk] * 4 + [edge] * 2 + [chunk] * 4,
        out_specs=[whole] * 2,
        scratch_shapes=[
            pltpu.VMEM((768, 1280), BF16),
            pltpu.VMEM((256, 1024), BF16),
            pltpu.VMEM((3, 256, 768), F32),
        ],
        compiler_params=params(20),
        cost_estimate=pl.CostEstimate(flops=4831838208, bytes_accessed=9000000, transcendentals=0),
        name="weight_grads",
    )(at, *chunks, top, bottom, *grads)


def ring(step):
    return [(i, (i + step) % 4) for i in range(4)]


def after(value, *others):
    return lax.optimization_barrier((value, *others))[0]


def gather(block, axis):
    return (
        block, lax.ppermute(block, axis, FIRST), lax.ppermute(block, axis, SECOND), lax.ppermute(block, axis, OPPOSITE)
    )


def edges(chunks):
    forward = [(i, i + 1) for i in range(7)]
    backward = [(j, i) for i, j in forward]
    last = jnp.stack([chunk[:, :, -LANES:] for chunk in chunks])
    first = jnp.stack([chunk[:, :, :LANES] for chunk in chunks])
    return (lax.ppermute(last, ("z", "core"), forward), lax.ppermute(first, ("z", "core"), backward))


def reduce_second(a, b, one_a, one_b, axis):
    two_a = lax.ppermute(a[1] + one_a[1], axis, SECOND)
    two_b = lax.ppermute(b[1] + one_b[1], axis, FIRST)
    return finish(a[0], one_a, two_a, b[0], one_b, two_b)


def fetch_weights(at, block):
    both = jnp.stack([block, lax.ppermute(block, "core", SWAP)])
    got = []
    for k in range(2):
        pairs = [
            ((z * 2 + s) * 4 + x, (((x + 2 * k + s) % 4) * 2 + s) * 4 + z)
            for z in range(4)
            for s in range(2)
            for x in range(4)
        ]
        got.append(lax.ppermute(both, ("z", "core", "x"), pairs))
    got = jnp.stack(got)
    return arrange_weights(at, got, lax.ppermute(got, "core", SWAP))


def step(images, kernel, upstream):
    at = jnp.stack([lax.axis_index(n) for n in ("z", "core", "x", "y")]).astype(jnp.int32)
    weights, turned = fetch_weights(at, kernel.reshape(9, 64, LANES))
    x, g = pack(images, upstream)
    x_chunks = gather(x, "y")
    g_chunks = gather(g, "x")

    x_sides = edges(x_chunks)
    g_sides = edges(g_chunks)
    out = conv((0, 1), at, x_chunks, x_sides, weights)
    out_a, out_b = out[:3], out[3:]
    out_one_a = lax.ppermute(out_a[2], "x", FIRST)
    out_one_b = lax.ppermute(out_b[2], "x", SECOND)
    grad_a = conv((0,), after(at, out_a[0]), g_chunks, g_sides, turned)
    grad_one_a = lax.ppermute(grad_a[2], "y", FIRST)
    grad_b = conv((1,), after(at, grad_a[0]), g_chunks, g_sides, turned)
    grad_one_b = lax.ppermute(grad_b[2], "y", SECOND)

    near, far = weight_grads(after(at, grad_b[0]), x_chunks, *x_sides, g_chunks)
    near = near + lax.ppermute(far, "core", SWAP)
    output_maps = reduce_second(out_a, out_b, out_one_a, out_one_b, "x")
    input_grad = reduce_second(grad_a, grad_b, grad_one_a, grad_one_b, "y")
    total = near[0]
    for k, turn in ((1, 1), (2, 3), (3, 2)):
        total = total + lax.ppermute(near[k], "z", ring(turn))
    cross = [(z * 4 + x, x * 4 + z) for z in range(4) for x in range(4)]
    kernel_grad = lax.ppermute(total, ("z", "x"), cross).reshape(3, 3, 64, LANES)
    return output_maps, input_grad, kernel_grad


def solution(mesh):
    fine = Mesh(mesh.devices.reshape(4, 2, 4, 4), ("z", "core", "x", "y"))
    row, col = ("z", "core"), ("x", "y")
    flat = P(None, row, col)
    taps = P(None, None, col, row)
    return jax.shard_map(step, mesh=fine, in_specs=(flat, taps, flat), out_specs=(flat, flat, taps), check_vma=False)
```

```python
import functools

import jax
import jax.numpy as jnp
from jax import lax
from jax.experimental import pallas as pl
from jax.experimental.pallas import tpu as pltpu
from jax.sharding import Mesh, PartitionSpec as P


W = 64
LANES = 128
F32 = jnp.float32
BF16 = jnp.bfloat16

FIRST = [(0, 1), (1, 0), (2, 3), (3, 2)]
SECOND = [(1, 2), (2, 1), (3, 0), (0, 3)]
OPPOSITE = [(i, (i + 2) % 4) for i in range(4)]
SWAP = [(0, 1), (1, 0)]


def params(mib):
    return pltpu.CompilerParams(vmem_limit_bytes=mib * 1024 * 1024)


def lane_of(shape):
    return lax.broadcasted_iota(jnp.int32, shape, len(shape) - 1)


def row_of(shape):
    return lax.broadcasted_iota(jnp.int32, shape, len(shape) - 2)


def place_of(member, position):
    odd = lax.rem(position, 2)
    apart = lax.rem(member - position + 4, 4)
    return jnp.where(apart == 0, 0, jnp.where(apart == 2, 3, jnp.where(apart == 1, 1 + odd, 2 - odd)))


def pack_kernel(x_ref, g_ref, x_out, g_out, rows_ref, mix_ref):
    low = lane_of((32, LANES)) < W
    for i, (t, q) in enumerate((t, q) for t in range(2) for q in range(4)):
        b = i % 2
        source, target = ((x_ref, x_out), (g_ref, g_out))[t]
        for side in range(2):
            flat = source[q + 4 * side].astype(F32)
            for p in range(32):
                rows_ref[b, side, :, p, :] = flat[:, p * LANES : (p + 1) * LANES]
        for h in range(8):
            first = rows_ref[b, 0, h]
            second = rows_ref[b, 1, h]
            mix_ref[b, h, pl.ds(0, 32, stride=2), :] = jnp.where(low, first, pltpu.roll(second, W, 1))
            mix_ref[b, h, pl.ds(1, 32, stride=2), :] = jnp.where(low, pltpu.roll(first, W, 1), second)
        for h in range(8):
            target[q, :, h * LANES : (h + 1) * LANES] = mix_ref[b, h].astype(BF16)


def pack(x, g):
    shape = jax.ShapeDtypeStruct((4, 64, 1024), BF16)
    near = pl.BlockSpec(memory_space=pltpu.VMEM)
    return pl.pallas_call(
        pack_kernel,
        out_shape=(shape, shape),
        in_specs=[near] * 2,
        out_specs=[near] * 2,
        scratch_shapes=[pltpu.VMEM((2, 2, 8, 32, LANES), F32), pltpu.VMEM((2, 8, 64, LANES), F32)],
        compiler_params=params(8),
        name="pack",
    )(x, g)


ROWS = ((1, 2, 3, 4), (5, 6, 7, 0))


def finish_kernel(own_a, one_a, two_a, own_b, one_b, two_b, o_hbm, given, mix_ref, rows_ref, out_sem):
    low = lane_of((32, LANES)) < W
    pieces = ((own_a, one_a, two_a), (own_b, one_b, two_b))

    def put(q, side):
        return pltpu.make_async_copy(given.at[q, side], o_hbm.at[q + 4 * side], out_sem.at[q, side])

    for q in range(4):
        b = q % 2
        for (own, one, two), rows in zip(pieces, ROWS):
            for j, h in enumerate(rows):
                lanes = slice(j * LANES, (j + 1) * LANES)
                mix_ref[b, h] = own[q, :, lanes] + one[0, q, :, lanes] + two[q, :, lanes]
        for h in range(8):
            even = mix_ref[b, h, pl.ds(0, 32, stride=2), :]
            odd = mix_ref[b, h, pl.ds(1, 32, stride=2), :]
            rows_ref[b, 0, h] = jnp.where(low, even, pltpu.roll(odd, W, 1))
            rows_ref[b, 1, h] = jnp.where(low, pltpu.roll(even, W, 1), odd)
        for side in range(2):
            for p in range(32):
                given[q, side, :, p * LANES : (p + 1) * LANES] = rows_ref[b, side, :, p, :].astype(BF16)
            put(q, side).start()
    for q in range(4):
        for side in range(2):
            put(q, side).wait()


def finish(*pieces):
    return pl.pallas_call(
        finish_kernel,
        out_shape=jax.ShapeDtypeStruct((8, 8, 4096), BF16),
        in_specs=[pl.BlockSpec(memory_space=pltpu.VMEM)] * 6,
        out_specs=pl.BlockSpec(memory_space=pl.ANY),
        scratch_shapes=[
            pltpu.VMEM((4, 2, 8, 4096), BF16),
            pltpu.VMEM((2, 8, 64, LANES), F32),
            pltpu.VMEM((2, 2, 8, 32, LANES), F32),
            pltpu.SemaphoreType.DMA((4, 2)),
        ],
        compiler_params=params(12),
        name="finish",
    )(*pieces)


def weights_kernel(at, mine, other, w_ref, wt_ref, whole):
    z, core, x, y = at[0], at[1], at[2], at[3]
    for ref, side in ((mine, core), (other, 1 - core)):
        for k in range(2):
            member = lax.rem(z + 8 - 2 * k - side, 4)
            rows = pl.ds(pl.multiple_of(place_of(member, x) * 64, 64), 64)
            for tap in range(9):
                for which, half in ((0, side), (1, 1 - side)):
                    lanes = pl.ds(pl.multiple_of(half * LANES, LANES), LANES)
                    whole[tap, rows, lanes] = ref[k, which, tap]
    listed, channel = row_of((256, 256)), lane_of((256, 256))
    order = jnp.where(
        (place_of(channel // 64, y) == listed // 64) & (channel % 64 == listed % 64), 1.0, 0.0
    ).astype(BF16)
    across = (((1,), (1,)), ((), ()))
    for tap in range(9):
        straight = lax.dot_general(whole[tap], order, across, preferred_element_type=F32).astype(BF16)
        turned = lax.dot_general(order, whole[tap], across, preferred_element_type=F32).astype(BF16)
        a, c = tap // 3, tap % 3
        w_ref[a, :, c * 256 : (c + 1) * 256] = straight
        wt_ref[2 - a, :, (2 - c) * 256 : (3 - c) * 256] = turned


def arrange_weights(at, mine, other):
    shape = jax.ShapeDtypeStruct((3, 256, 768), BF16)
    return pl.pallas_call(
        weights_kernel,
        out_shape=(shape, shape),
        in_specs=[pl.BlockSpec(memory_space=pltpu.SMEM)] + [pl.BlockSpec(memory_space=pltpu.VMEM)] * 2,
        out_specs=[pl.BlockSpec(memory_space=pltpu.VMEM)] * 2,
        scratch_shapes=[pltpu.VMEM((9, 256, 256), BF16)],
        compiler_params=params(20),
        name="weights",
    )(at, mine, other)


def lay_shifted(chunks, top, bottom, rows, shifted):
    column = lane_of((64, LANES)) % W
    not_first = jnp.where(column == 0, 0.0, 1.0).astype(BF16)
    not_last = jnp.where(column == W - 1, 0.0, 1.0).astype(BF16)
    for k in range(4):
        at = k * 64
        for j, h in enumerate(rows):
            if h == -1:
                tile = top[k, 0]
            elif h == 8:
                tile = bottom[k, 0]
            else:
                tile = chunks[k][0, :, h * LANES : (h + 1) * LANES]
            lanes = slice(j * LANES, (j + 1) * LANES)
            shifted[at : at + 64, lanes] = pltpu.roll(tile, 1, 1) * not_first
            shifted[256 + at : 320 + at, lanes] = tile
            shifted[512 + at : 576 + at, lanes] = pltpu.roll(tile, LANES - 1, 1) * not_last


def conv_kernel(halves, rows, at, c0, c1, c2, c3, *refs):
    edged = 1 in halves
    top, bottom = refs[:2] if edged else (None, None)
    refs = refs[2 * edged :]
    w_ref, shifted = refs[0], refs[-1]
    lay_shifted((c0, c1, c2, c3), top, bottom, rows, shifted)
    for i, half in enumerate(halves):
        own, following, send = refs[1 + 3 * i : 4 + 3 * i]
        for n in range(2):
            part = None
            for a in range(3):
                places = [rows.index(h - 1 + a) for h in ROWS[half][2 * n : 2 * n + 2]]
                source = jnp.concatenate([shifted[:, j * LANES : (j + 1) * LANES] for j in places], axis=1)
                term = jnp.dot(w_ref[a], source, preferred_element_type=F32)
                part = term if part is None else part + term
            lanes = slice(n * 256, (n + 1) * 256)
            own[0, :, lanes] = part[0:64]
            pair = (following.at[0], send.at[0, 0]) if half else (send.at[0, 0], following.at[0])
            pair[0][:, lanes] = part[64:128]
            pair[1][:, lanes] = part[128:192]
            send[1, 0, :, lanes] = part[192:256]


def conv(halves, at, chunks, sides, weights):
    rows = {(0,): (0, 1, 2, 3, 4, 5), (1,): (4, 5, 6, 7, 8, -1, 0, 1)}.get(halves, tuple(range(-1, 9)))
    single = jax.ShapeDtypeStruct((4, 64, 512), F32)
    double = jax.ShapeDtypeStruct((2, 4, 64, 512), F32)
    chunk = pl.BlockSpec((1, 64, 1024), lambda q: (q, 0, 0))
    edge = pl.BlockSpec((4, 1, 64, LANES), lambda q: (0, q, 0, 0))
    one = pl.BlockSpec((1, 64, 512), lambda q: (q, 0, 0))
    two = pl.BlockSpec((2, 1, 64, 512), lambda q: (0, q, 0, 0))
    sides = sides if 1 in halves else ()
    return pl.pallas_call(
        functools.partial(conv_kernel, halves, rows),
        out_shape=(single, single, double) * len(halves),
        grid=(4,),
        in_specs=[pl.BlockSpec(memory_space=pltpu.SMEM)]
        + [chunk] * 4
        + [edge] * len(sides)
        + [pl.BlockSpec((3, 256, 768), lambda q: (0, 0, 0))],
        out_specs=[one, one, two] * len(halves),
        scratch_shapes=[pltpu.VMEM((768, len(rows) * LANES), BF16)],
        compiler_params=params(16),
        cost_estimate=pl.CostEstimate(
            flops=2415919104 * len(halves), bytes_accessed=6000000 * len(halves), transcendentals=0
        ),
    )(at, *chunks, *sides, weights)


def kernel_grad_kernel(at, x0, x1, x2, x3, top, bottom, g0, g1, g2, g3, mine, other, shifted, grads, total):
    z, core, x, y = at[0], at[1], at[2], at[3]
    q = pl.program_id(0)
    lay_shifted((x0, x1, x2, x3), top, bottom, range(-1, 9), shifted)
    for k, g_ref in enumerate((g0, g1, g2, g3)):
        grads[k * 64 : (k + 1) * 64, :] = g_ref[0]

    @pl.when(q == 0)
    def _():
        total[...] = jnp.zeros_like(total)

    for a in range(3):
        total[a] += lax.dot_general(
            grads[...],
            shifted[:, a * LANES : a * LANES + 1024],
            (((1,), (1,)), ((), ())),
            preferred_element_type=F32,
        )

    @pl.when(q == 3)
    def _():
        for half, o_ref in ((core, mine), (1 - core, other)):
            second = jnp.where(half == y // 2, 0, 1)
            straight = second == lax.rem(y, 2)
            for k in range(4):
                member = lax.rem(z + (0, 1, 3, 2)[k], 4)
                rows = pl.ds(pl.multiple_of(place_of(member, x) * 64, 64), 64)
                for a in range(3):
                    for c in range(3):
                        lanes = pl.ds(pl.multiple_of(c * 256 + second * LANES, LANES), LANES)
                        tile = total[a, rows, lanes]
                        o_ref[k, a * 3 + c] = jnp.where(straight, tile, pltpu.roll(tile, W, 1))


def weight_grads(at, chunks, top, bottom, grads):
    shape = jax.ShapeDtypeStruct((4, 9, 64, LANES), F32)
    chunk = pl.BlockSpec((1, 64, 1024), lambda q: (q, 0, 0))
    edge = pl.BlockSpec((4, 1, 64, LANES), lambda q: (0, q, 0, 0))
    whole = pl.BlockSpec((4, 9, 64, LANES), lambda q: (0, 0, 0, 0))
    return pl.pallas_call(
        kernel_grad_kernel,
        out_shape=(shape,) * 2,
        grid=(4,),
        in_specs=[pl.BlockSpec(memory_space=pltpu.SMEM)] + [chunk] * 4 + [edge] * 2 + [chunk] * 4,
        out_specs=[whole] * 2,
        scratch_shapes=[
            pltpu.VMEM((768, 1280), BF16),
            pltpu.VMEM((256, 1024), BF16),
            pltpu.VMEM((3, 256, 768), F32),
        ],
        compiler_params=params(20),
        cost_estimate=pl.CostEstimate(flops=4831838208, bytes_accessed=9000000, transcendentals=0),
        name="weight_grads",
    )(at, *chunks, top, bottom, *grads)


def ring(step):
    return [(i, (i + step) % 4) for i in range(4)]


def after(value, *others):
    return lax.optimization_barrier((value, *others))[0]


def gather(block, axis):
    return (
        block, lax.ppermute(block, axis, FIRST), lax.ppermute(block, axis, SECOND), lax.ppermute(block, axis, OPPOSITE)
    )


def edges(chunks):
    forward = [(i, i + 1) for i in range(7)]
    backward = [(j, i) for i, j in forward]
    last = jnp.stack([chunk[:, :, -LANES:] for chunk in chunks])
    first = jnp.stack([chunk[:, :, :LANES] for chunk in chunks])
    return (lax.ppermute(last, ("z", "core"), forward), lax.ppermute(first, ("z", "core"), backward))


def reduce_second(a, b, one_a, one_b, axis):
    two_a = lax.ppermute(a[1] + one_a[1], axis, SECOND)
    two_b = lax.ppermute(b[1] + one_b[1], axis, FIRST)
    return finish(a[0], one_a, two_a, b[0], one_b, two_b)


def fetch_weights(at, block):
    both = jnp.stack([block, lax.ppermute(block, "core", SWAP)])
    got = []
    for k in range(2):
        pairs = [
            ((z * 2 + s) * 4 + x, (((x + 2 * k + s) % 4) * 2 + s) * 4 + z)
            for z in range(4)
            for s in range(2)
            for x in range(4)
        ]
        got.append(lax.ppermute(both, ("z", "core", "x"), pairs))
    got = jnp.stack(got)
    return arrange_weights(at, got, lax.ppermute(got, "core", SWAP))


def step(images, kernel, upstream):
    at = jnp.stack([lax.axis_index(n) for n in ("z", "core", "x", "y")]).astype(jnp.int32)
    weights, turned = fetch_weights(at, kernel.reshape(9, 64, LANES))
    x, g = pack(images, upstream)
    x_chunks = gather(x, "y")
    g_chunks = gather(g, "x")

    x_sides = edges(x_chunks)
    g_sides = edges(g_chunks)
    out = conv((0, 1), at, x_chunks, x_sides, weights)
    out_a, out_b = out[:3], out[3:]
    out_one_a = lax.ppermute(out_a[2], "x", FIRST)
    out_one_b = lax.ppermute(out_b[2], "x", SECOND)
    grad_a = conv((0,), after(at, out_a[0]), g_chunks, g_sides, turned)
    grad_one_a = lax.ppermute(grad_a[2], "y", FIRST)
    grad_b = conv((1,), after(at, grad_a[0]), g_chunks, g_sides, turned)
    grad_one_b = lax.ppermute(grad_b[2], "y", SECOND)

    near, far = weight_grads(after(at, grad_b[0]), x_chunks, *x_sides, g_chunks)
    near = near + lax.ppermute(far, "core", SWAP)
    output_maps = reduce_second(out_a, out_b, out_one_a, out_one_b, "x")
    input_grad = reduce_second(grad_a, grad_b, grad_one_a, grad_one_b, "y")
    total = near[0]
    for k, turn in ((1, 1), (2, 3), (3, 2)):
        total = total + lax.ppermute(near[k], "z", ring(turn))
    cross = [(z * 4 + x, x * 4 + z) for z in range(4) for x in range(4)]
    kernel_grad = lax.ppermute(total, ("z", "x"), cross).reshape(3, 3, 64, LANES)
    return output_maps, input_grad, kernel_grad


def solution(mesh):
    fine = Mesh(mesh.devices.reshape(4, 2, 4, 4), ("z", "core", "x", "y"))
    row, col = ("z", "core"), ("x", "y")
    flat = P(None, row, col)
    taps = P(None, None, col, row)
    return jax.shard_map(step, mesh=fine, in_specs=(flat, taps, flat), out_specs=(flat, flat, taps), check_vma=False)
```

```python
import functools

import jax
import jax.numpy as jnp
from jax import lax
from jax.experimental import pallas as pl
from jax.experimental.pallas import tpu as pltpu
from jax.sharding import Mesh, PartitionSpec as P


W = 64
LANES = 128
F32 = jnp.float32
BF16 = jnp.bfloat16

FIRST = [(0, 1), (1, 0), (2, 3), (3, 2)]
SECOND = [(1, 2), (2, 1), (3, 0), (0, 3)]
OPPOSITE = [(i, (i + 2) % 4) for i in range(4)]
SWAP = [(0, 1), (1, 0)]


def params(mib):
    return pltpu.CompilerParams(vmem_limit_bytes=mib * 1024 * 1024)


def lane_of(shape):
    return lax.broadcasted_iota(jnp.int32, shape, len(shape) - 1)


def row_of(shape):
    return lax.broadcasted_iota(jnp.int32, shape, len(shape) - 2)


def place_of(member, position):
    odd = lax.rem(position, 2)
    apart = lax.rem(member - position + 4, 4)
    return jnp.where(apart == 0, 0, jnp.where(apart == 2, 3, jnp.where(apart == 1, 1 + odd, 2 - odd)))


def pack_kernel(x_ref, g_ref, x_out, g_out, rows_ref, mix_ref):
    low = lane_of((32, LANES)) < W
    for i, (t, q) in enumerate((t, q) for t in range(2) for q in range(4)):
        b = i % 2
        source, target = ((x_ref, x_out), (g_ref, g_out))[t]
        for side in range(2):
            flat = source[q + 4 * side].astype(F32)
            for p in range(32):
                rows_ref[b, side, :, p, :] = flat[:, p * LANES : (p + 1) * LANES]
        for h in range(8):
            first = rows_ref[b, 0, h]
            second = rows_ref[b, 1, h]
            mix_ref[b, h, pl.ds(0, 32, stride=2), :] = jnp.where(low, first, pltpu.roll(second, W, 1))
            mix_ref[b, h, pl.ds(1, 32, stride=2), :] = jnp.where(low, pltpu.roll(first, W, 1), second)
        for h in range(8):
            target[q, :, h * LANES : (h + 1) * LANES] = mix_ref[b, h].astype(BF16)


def pack(x, g):
    shape = jax.ShapeDtypeStruct((4, 64, 1024), BF16)
    near = pl.BlockSpec(memory_space=pltpu.VMEM)
    return pl.pallas_call(
        pack_kernel,
        out_shape=(shape, shape),
        in_specs=[near] * 2,
        out_specs=[near] * 2,
        scratch_shapes=[pltpu.VMEM((2, 2, 8, 32, LANES), F32), pltpu.VMEM((2, 8, 64, LANES), F32)],
        compiler_params=params(8),
        name="pack",
    )(x, g)


ROWS = ((1, 2, 3, 4), (5, 6, 7, 0))


def finish_kernel(own_a, one_a, two_a, own_b, one_b, two_b, o_hbm, given, mix_ref, rows_ref, out_sem):
    low = lane_of((32, LANES)) < W
    pieces = ((own_a, one_a, two_a), (own_b, one_b, two_b))

    def put(q, side):
        return pltpu.make_async_copy(given.at[q, side], o_hbm.at[q + 4 * side], out_sem.at[q, side])

    for q in range(4):
        b = q % 2
        for (own, one, two), rows in zip(pieces, ROWS):
            for j, h in enumerate(rows):
                lanes = slice(j * LANES, (j + 1) * LANES)
                mix_ref[b, h] = own[q, :, lanes] + one[0, q, :, lanes] + two[q, :, lanes]
        for h in range(8):
            even = mix_ref[b, h, pl.ds(0, 32, stride=2), :]
            odd = mix_ref[b, h, pl.ds(1, 32, stride=2), :]
            rows_ref[b, 0, h] = jnp.where(low, even, pltpu.roll(odd, W, 1))
            rows_ref[b, 1, h] = jnp.where(low, pltpu.roll(even, W, 1), odd)
        for side in range(2):
            for p in range(32):
                given[q, side, :, p * LANES : (p + 1) * LANES] = rows_ref[b, side, :, p, :].astype(BF16)
            put(q, side).start()
    for q in range(4):
        for side in range(2):
            put(q, side).wait()


def finish(*pieces):
    return pl.pallas_call(
        finish_kernel,
        out_shape=jax.ShapeDtypeStruct((8, 8, 4096), BF16),
        in_specs=[pl.BlockSpec(memory_space=pltpu.VMEM)] * 6,
        out_specs=pl.BlockSpec(memory_space=pl.ANY),
        scratch_shapes=[
            pltpu.VMEM((4, 2, 8, 4096), BF16),
            pltpu.VMEM((2, 8, 64, LANES), F32),
            pltpu.VMEM((2, 2, 8, 32, LANES), F32),
            pltpu.SemaphoreType.DMA((4, 2)),
        ],
        compiler_params=params(12),
        name="finish",
    )(*pieces)


def listed(position, k):
    odd = lax.rem(position, 2)
    return lax.rem(position + (0, 1 + 2 * odd, 3 - 2 * odd, 2)[k], 4)


def route_kernel(at, b0, b1, b2, b3, o0, o1, o2, o3, held):
    for k, ref in enumerate((b0, b1, b2, b3)):
        held[k] = ref[...]
    for k, ref in enumerate((o0, o1, o2, o3)):
        ref[...] = held[place_of(listed(at[2], k), at[0])]


def route_weights(at, blocks):
    shape = jax.ShapeDtypeStruct((9, 64, LANES), BF16)
    near = pl.BlockSpec(memory_space=pltpu.VMEM)
    return pl.pallas_call(
        route_kernel,
        out_shape=(shape,) * 4,
        in_specs=[pl.BlockSpec(memory_space=pltpu.SMEM)] + [near] * 4,
        out_specs=[near] * 4,
        scratch_shapes=[pltpu.VMEM((4, 9, 64, LANES), BF16)],
        compiler_params=params(4),
        name="route",
    )(at, *blocks)


def weights_kernel(at, mine, other, w_ref, wt_ref, whole):
    core, y = at[1], at[3]
    for ref, side in ((mine, core), (other, 1 - core)):
        lanes = pl.ds(pl.multiple_of(side * LANES, LANES), LANES)
        for k in range(4):
            for tap in range(9):
                whole[tap, k * 64 : (k + 1) * 64, lanes] = ref[k, tap]
    place, channel = row_of((256, 256)), lane_of((256, 256))
    order = jnp.where(
        (place_of(channel // 64, y) == place // 64) & (channel % 64 == place % 64), 1.0, 0.0
    ).astype(BF16)
    across = (((1,), (1,)), ((), ()))
    for tap in range(9):
        straight = lax.dot_general(whole[tap], order, across, preferred_element_type=F32).astype(BF16)
        turned = lax.dot_general(order, whole[tap], across, preferred_element_type=F32).astype(BF16)
        a, c = tap // 3, tap % 3
        w_ref[a, :, c * 256 : (c + 1) * 256] = straight
        wt_ref[2 - a, :, (2 - c) * 256 : (3 - c) * 256] = turned


def arrange_weights(at, mine, other):
    shape = jax.ShapeDtypeStruct((3, 256, 768), BF16)
    return pl.pallas_call(
        weights_kernel,
        out_shape=(shape, shape),
        in_specs=[pl.BlockSpec(memory_space=pltpu.SMEM)] + [pl.BlockSpec(memory_space=pltpu.VMEM)] * 2,
        out_specs=[pl.BlockSpec(memory_space=pltpu.VMEM)] * 2,
        scratch_shapes=[pltpu.VMEM((9, 256, 256), BF16)],
        compiler_params=params(20),
        name="weights",
    )(at, mine, other)


def lay_shifted(chunks, top, bottom, rows, shifted):
    column = lane_of((64, LANES)) % W
    not_first = jnp.where(column == 0, 0.0, 1.0).astype(BF16)
    not_last = jnp.where(column == W - 1, 0.0, 1.0).astype(BF16)
    for k in range(4):
        at = k * 64
        for j, h in enumerate(rows):
            if h == -1:
                tile = top[k, 0]
            elif h == 8:
                tile = bottom[k, 0]
            else:
                tile = chunks[k][0, :, h * LANES : (h + 1) * LANES]
            lanes = slice(j * LANES, (j + 1) * LANES)
            shifted[at : at + 64, lanes] = pltpu.roll(tile, 1, 1) * not_first
            shifted[256 + at : 320 + at, lanes] = tile
            shifted[512 + at : 576 + at, lanes] = pltpu.roll(tile, LANES - 1, 1) * not_last


def conv_kernel(halves, rows, at, c0, c1, c2, c3, *refs):
    edged = 1 in halves
    top, bottom = refs[:2] if edged else (None, None)
    refs = refs[2 * edged :]
    w_ref, shifted = refs[0], refs[-1]
    lay_shifted((c0, c1, c2, c3), top, bottom, rows, shifted)
    for i, half in enumerate(halves):
        own, following, send = refs[1 + 3 * i : 4 + 3 * i]
        for n in range(2):
            part = None
            for a in range(3):
                places = [rows.index(h - 1 + a) for h in ROWS[half][2 * n : 2 * n + 2]]
                source = jnp.concatenate([shifted[:, j * LANES : (j + 1) * LANES] for j in places], axis=1)
                term = jnp.dot(w_ref[a], source, preferred_element_type=F32)
                part = term if part is None else part + term
            lanes = slice(n * 256, (n + 1) * 256)
            own[0, :, lanes] = part[0:64]
            pair = (following.at[0], send.at[0, 0]) if half else (send.at[0, 0], following.at[0])
            pair[0][:, lanes] = part[64:128]
            pair[1][:, lanes] = part[128:192]
            send[1, 0, :, lanes] = part[192:256]


def conv(halves, at, chunks, sides, weights):
    rows = {(0,): (0, 1, 2, 3, 4, 5), (1,): (4, 5, 6, 7, 8, -1, 0, 1)}.get(halves, tuple(range(-1, 9)))
    single = jax.ShapeDtypeStruct((4, 64, 512), F32)
    double = jax.ShapeDtypeStruct((2, 4, 64, 512), F32)
    chunk = pl.BlockSpec((1, 64, 1024), lambda q: (q, 0, 0))
    edge = pl.BlockSpec((4, 1, 64, LANES), lambda q: (0, q, 0, 0))
    one = pl.BlockSpec((1, 64, 512), lambda q: (q, 0, 0))
    two = pl.BlockSpec((2, 1, 64, 512), lambda q: (0, q, 0, 0))
    sides = sides if 1 in halves else ()
    return pl.pallas_call(
        functools.partial(conv_kernel, halves, rows),
        out_shape=(single, single, double) * len(halves),
        grid=(4,),
        in_specs=[pl.BlockSpec(memory_space=pltpu.SMEM)]
        + [chunk] * 4
        + [edge] * len(sides)
        + [pl.BlockSpec((3, 256, 768), lambda q: (0, 0, 0))],
        out_specs=[one, one, two] * len(halves),
        scratch_shapes=[pltpu.VMEM((768, len(rows) * LANES), BF16)],
        compiler_params=params(16),
        cost_estimate=pl.CostEstimate(
            flops=2415919104 * len(halves), bytes_accessed=6000000 * len(halves), transcendentals=0
        ),
    )(at, *chunks, *sides, weights)


def kernel_grad_kernel(at, x0, x1, x2, x3, top, bottom, g0, g1, g2, g3, mine, other, shifted, grads, total):
    z, core, x, y = at[0], at[1], at[2], at[3]
    q = pl.program_id(0)
    lay_shifted((x0, x1, x2, x3), top, bottom, range(-1, 9), shifted)
    for k, g_ref in enumerate((g0, g1, g2, g3)):
        grads[k * 64 : (k + 1) * 64, :] = g_ref[0]

    @pl.when(q == 0)
    def _():
        total[...] = jnp.zeros_like(total)

    for a in range(3):
        total[a] += lax.dot_general(
            grads[...],
            shifted[:, a * LANES : a * LANES + 1024],
            (((1,), (1,)), ((), ())),
            preferred_element_type=F32,
        )

    @pl.when(q == 3)
    def _():
        for half, o_ref in ((core, mine), (1 - core, other)):
            second = jnp.where(half == y // 2, 0, 1)
            straight = second == lax.rem(y, 2)
            for k in range(4):
                member = lax.rem(z + (0, 1, 3, 2)[k], 4)
                rows = pl.ds(pl.multiple_of(place_of(member, x) * 64, 64), 64)
                for a in range(3):
                    for c in range(3):
                        lanes = pl.ds(pl.multiple_of(c * 256 + second * LANES, LANES), LANES)
                        tile = total[a, rows, lanes]
                        o_ref[k, a * 3 + c] = jnp.where(straight, tile, pltpu.roll(tile, W, 1))


def weight_grads(at, chunks, top, bottom, grads):
    shape = jax.ShapeDtypeStruct((4, 9, 64, LANES), F32)
    chunk = pl.BlockSpec((1, 64, 1024), lambda q: (q, 0, 0))
    edge = pl.BlockSpec((4, 1, 64, LANES), lambda q: (0, q, 0, 0))
    whole = pl.BlockSpec((4, 9, 64, LANES), lambda q: (0, 0, 0, 0))
    return pl.pallas_call(
        kernel_grad_kernel,
        out_shape=(shape,) * 2,
        grid=(4,),
        in_specs=[pl.BlockSpec(memory_space=pltpu.SMEM)] + [chunk] * 4 + [edge] * 2 + [chunk] * 4,
        out_specs=[whole] * 2,
        scratch_shapes=[
            pltpu.VMEM((768, 1280), BF16),
            pltpu.VMEM((256, 1024), BF16),
            pltpu.VMEM((3, 256, 768), F32),
        ],
        compiler_params=params(20),
        cost_estimate=pl.CostEstimate(flops=4831838208, bytes_accessed=9000000, transcendentals=0),
        name="weight_grads",
    )(at, *chunks, top, bottom, *grads)


def ring(step):
    return [(i, (i + step) % 4) for i in range(4)]


def after(value, *others):
    return lax.optimization_barrier((value, *others))[0]


def gather(block, axis):
    return (
        block, lax.ppermute(block, axis, FIRST), lax.ppermute(block, axis, SECOND), lax.ppermute(block, axis, OPPOSITE)
    )


def edges(chunks):
    forward = [(i, i + 1) for i in range(7)]
    backward = [(j, i) for i, j in forward]
    last = jnp.stack([chunk[:, :, -LANES:] for chunk in chunks])
    first = jnp.stack([chunk[:, :, :LANES] for chunk in chunks])
    return (lax.ppermute(last, ("z", "core"), forward), lax.ppermute(first, ("z", "core"), backward))


def reduce_second(a, b, one_a, one_b, axis):
    two_a = lax.ppermute(a[1] + one_a[1], axis, SECOND)
    two_b = lax.ppermute(b[1] + one_b[1], axis, FIRST)
    return finish(a[0], one_a, two_a, b[0], one_b, two_b)


def fetch_weights(at, block):
    along_z = gather(block, "z")
    own, first, second, far = route_weights(at, along_z)
    got = (own, lax.ppermute(first, "x", FIRST), lax.ppermute(second, "x", SECOND), lax.ppermute(far, "x", OPPOSITE))
    got = jnp.stack(got)
    return arrange_weights(at, got, lax.ppermute(got, "core", SWAP))


def step(images, kernel, upstream):
    at = jnp.stack([lax.axis_index(n) for n in ("z", "core", "x", "y")]).astype(jnp.int32)
    weights, turned = fetch_weights(at, kernel.reshape(9, 64, LANES))
    x, g = pack(images, upstream)
    x_chunks = gather(x, "y")
    g_chunks = gather(g, "x")

    x_sides = edges(x_chunks)
    g_sides = edges(g_chunks)
    out = conv((0, 1), at, x_chunks, x_sides, weights)
    out_a, out_b = out[:3], out[3:]
    out_one_a = lax.ppermute(out_a[2], "x", FIRST)
    out_one_b = lax.ppermute(out_b[2], "x", SECOND)
    grad_a = conv((0,), after(at, out_a[0]), g_chunks, g_sides, turned)
    grad_one_a = lax.ppermute(grad_a[2], "y", FIRST)
    grad_b = conv((1,), after(at, grad_a[0]), g_chunks, g_sides, turned)
    grad_one_b = lax.ppermute(grad_b[2], "y", SECOND)

    near, far = weight_grads(after(at, grad_b[0]), x_chunks, *x_sides, g_chunks)
    near = near + lax.ppermute(far, "core", SWAP)
    output_maps = reduce_second(out_a, out_b, out_one_a, out_one_b, "x")
    input_grad = reduce_second(grad_a, grad_b, grad_one_a, grad_one_b, "y")
    total = near[0]
    for k, turn in ((1, 1), (2, 3), (3, 2)):
        total = total + lax.ppermute(near[k], "z", ring(turn))
    cross = [(z * 4 + x, x * 4 + z) for z in range(4) for x in range(4)]
    kernel_grad = lax.ppermute(total, ("z", "x"), cross).reshape(3, 3, 64, LANES)
    return output_maps, input_grad, kernel_grad


def solution(mesh):
    fine = Mesh(mesh.devices.reshape(4, 2, 4, 4), ("z", "core", "x", "y"))
    row, col = ("z", "core"), ("x", "y")
    flat = P(None, row, col)
    taps = P(None, None, col, row)
    return jax.shard_map(step, mesh=fine, in_specs=(flat, taps, flat), out_specs=(flat, flat, taps), check_vma=False)
```

```python
import functools

import jax
import jax.numpy as jnp
from jax import lax
from jax.experimental import pallas as pl
from jax.experimental.pallas import tpu as pltpu
from jax.sharding import Mesh, PartitionSpec as P


W = 64
LANES = 128
F32 = jnp.float32
BF16 = jnp.bfloat16

FIRST = [(0, 1), (1, 0), (2, 3), (3, 2)]
SECOND = [(1, 2), (2, 1), (3, 0), (0, 3)]
OPPOSITE = [(i, (i + 2) % 4) for i in range(4)]
SWAP = [(0, 1), (1, 0)]


def params(mib):
    return pltpu.CompilerParams(vmem_limit_bytes=mib * 1024 * 1024)


def lane_of(shape):
    return lax.broadcasted_iota(jnp.int32, shape, len(shape) - 1)


def row_of(shape):
    return lax.broadcasted_iota(jnp.int32, shape, len(shape) - 2)


def place_of(member, position):
    odd = lax.rem(position, 2)
    apart = lax.rem(member - position + 4, 4)
    return jnp.where(apart == 0, 0, jnp.where(apart == 2, 3, jnp.where(apart == 1, 1 + odd, 2 - odd)))


def pack_kernel(x_ref, g_ref, x_out, g_out, rows_ref, mix_ref):
    low = lane_of((32, LANES)) < W
    for i, (t, q) in enumerate((t, q) for t in range(2) for q in range(4)):
        b = i % 2
        source, target = ((x_ref, x_out), (g_ref, g_out))[t]
        for side in range(2):
            flat = source[q + 4 * side].astype(F32)
            for p in range(32):
                rows_ref[b, side, :, p, :] = flat[:, p * LANES : (p + 1) * LANES]
        for h in range(8):
            first = rows_ref[b, 0, h]
            second = rows_ref[b, 1, h]
            mix_ref[b, h, pl.ds(0, 32, stride=2), :] = jnp.where(low, first, pltpu.roll(second, W, 1))
            mix_ref[b, h, pl.ds(1, 32, stride=2), :] = jnp.where(low, pltpu.roll(first, W, 1), second)
        for h in range(8):
            target[q, :, h * LANES : (h + 1) * LANES] = mix_ref[b, h].astype(BF16)


def pack(x, g):
    shape = jax.ShapeDtypeStruct((4, 64, 1024), BF16)
    near = pl.BlockSpec(memory_space=pltpu.VMEM)
    return pl.pallas_call(
        pack_kernel,
        out_shape=(shape, shape),
        in_specs=[near] * 2,
        out_specs=[near] * 2,
        scratch_shapes=[pltpu.VMEM((2, 2, 8, 32, LANES), F32), pltpu.VMEM((2, 8, 64, LANES), F32)],
        compiler_params=params(8),
        name="pack",
    )(x, g)


ROWS = ((1, 2, 3, 4), (5, 6, 7, 0))


def finish_kernel(own_a, one_a, two_a, own_b, one_b, two_b, *refs):
    given, mix_ref, rows_ref, out_sem, more_sem = refs[-5:]
    o_hbm = refs[-6] if len(refs) == 6 else refs[1]
    more = pltpu.make_async_copy(refs[0], refs[2], more_sem) if len(refs) == 8 else None
    if more is not None:
        more.start()
    low = lane_of((32, LANES)) < W
    pieces = ((own_a, one_a, two_a), (own_b, one_b, two_b))

    def put(q, side):
        return pltpu.make_async_copy(given.at[q, side], o_hbm.at[q + 4 * side], out_sem.at[q, side])

    for q in range(4):
        b = q % 2
        for (own, one, two), rows in zip(pieces, ROWS):
            for j, h in enumerate(rows):
                lanes = slice(j * LANES, (j + 1) * LANES)
                mix_ref[b, h] = own[q, :, lanes] + one[0, q, :, lanes] + two[q, :, lanes]
        for h in range(8):
            even = mix_ref[b, h, pl.ds(0, 32, stride=2), :]
            odd = mix_ref[b, h, pl.ds(1, 32, stride=2), :]
            rows_ref[b, 0, h] = jnp.where(low, even, pltpu.roll(odd, W, 1))
            rows_ref[b, 1, h] = jnp.where(low, pltpu.roll(even, W, 1), odd)
        for side in range(2):
            for p in range(32):
                given[q, side, :, p * LANES : (p + 1) * LANES] = rows_ref[b, side, :, p, :].astype(BF16)
            put(q, side).start()
    for q in range(4):
        for side in range(2):
            put(q, side).wait()
    if more is not None:
        more.wait()


def finish(*pieces):
    shapes = [jax.ShapeDtypeStruct((8, 8, 4096), BF16)]
    shapes += [jax.ShapeDtypeStruct(piece.shape, piece.dtype) for piece in pieces[6:]]
    specs = [pl.BlockSpec(memory_space=pl.ANY)] * len(shapes)
    return pl.pallas_call(
        finish_kernel,
        out_shape=shapes if len(shapes) > 1 else shapes[0],
        in_specs=[pl.BlockSpec(memory_space=pltpu.VMEM)] * len(pieces),
        out_specs=specs if len(shapes) > 1 else specs[0],
        scratch_shapes=[
            pltpu.VMEM((4, 2, 8, 4096), BF16),
            pltpu.VMEM((2, 8, 64, LANES), F32),
            pltpu.VMEM((2, 2, 8, 32, LANES), F32),
            pltpu.SemaphoreType.DMA((4, 2)),
            pltpu.SemaphoreType.DMA,
        ],
        compiler_params=params(12),
        name="finish",
    )(*pieces)


def listed(position, k):
    odd = lax.rem(position, 2)
    return lax.rem(position + (0, 1 + 2 * odd, 3 - 2 * odd, 2)[k], 4)


def route_kernel(at, b0, b1, b2, b3, o0, o1, o2, o3, held):
    for k, ref in enumerate((b0, b1, b2, b3)):
        held[k] = ref[...]
    for k, ref in enumerate((o0, o1, o2, o3)):
        ref[...] = held[place_of(listed(at[2], k), at[0])]


def route_weights(at, blocks):
    shape = jax.ShapeDtypeStruct((9, 64, LANES), BF16)
    near = pl.BlockSpec(memory_space=pltpu.VMEM)
    return pl.pallas_call(
        route_kernel,
        out_shape=(shape,) * 4,
        in_specs=[pl.BlockSpec(memory_space=pltpu.SMEM)] + [near] * 4,
        out_specs=[near] * 4,
        scratch_shapes=[pltpu.VMEM((4, 9, 64, LANES), BF16)],
        compiler_params=params(4),
        name="route",
    )(at, *blocks)


def weights_kernel(at, mine, other, w_ref, wt_ref, whole):
    core, y = at[1], at[3]
    for ref, side in ((mine, core), (other, 1 - core)):
        lanes = pl.ds(pl.multiple_of(side * LANES, LANES), LANES)
        for k in range(4):
            for tap in range(9):
                whole[tap, k * 64 : (k + 1) * 64, lanes] = ref[k, tap]
    place, channel = row_of((256, 256)), lane_of((256, 256))
    order = jnp.where(
        (place_of(channel // 64, y) == place // 64) & (channel % 64 == place % 64), 1.0, 0.0
    ).astype(BF16)
    across = (((1,), (1,)), ((), ()))
    for tap in range(9):
        straight = lax.dot_general(whole[tap], order, across, preferred_element_type=F32).astype(BF16)
        turned = lax.dot_general(order, whole[tap], across, preferred_element_type=F32).astype(BF16)
        a, c = tap // 3, tap % 3
        w_ref[a, :, c * 256 : (c + 1) * 256] = straight
        wt_ref[2 - a, :, (2 - c) * 256 : (3 - c) * 256] = turned


def arrange_weights(at, mine, other):
    shape = jax.ShapeDtypeStruct((3, 256, 768), BF16)
    return pl.pallas_call(
        weights_kernel,
        out_shape=(shape, shape),
        in_specs=[pl.BlockSpec(memory_space=pltpu.SMEM)] + [pl.BlockSpec(memory_space=pltpu.VMEM)] * 2,
        out_specs=[pl.BlockSpec(memory_space=pltpu.VMEM)] * 2,
        scratch_shapes=[pltpu.VMEM((9, 256, 256), BF16)],
        compiler_params=params(20),
        name="weights",
    )(at, mine, other)


def lay_shifted(chunks, top, bottom, rows, shifted):
    column = lane_of((64, LANES)) % W
    not_first = jnp.where(column == 0, 0.0, 1.0).astype(BF16)
    not_last = jnp.where(column == W - 1, 0.0, 1.0).astype(BF16)
    for k in range(4):
        at = k * 64
        for j, h in enumerate(rows):
            if h == -1:
                tile = top[k, 0]
            elif h == 8:
                tile = bottom[k, 0]
            else:
                tile = chunks[k][0, :, h * LANES : (h + 1) * LANES]
            lanes = slice(j * LANES, (j + 1) * LANES)
            shifted[at : at + 64, lanes] = pltpu.roll(tile, 1, 1) * not_first
            shifted[256 + at : 320 + at, lanes] = tile
            shifted[512 + at : 576 + at, lanes] = pltpu.roll(tile, LANES - 1, 1) * not_last


def conv_kernel(halves, rows, at, c0, c1, c2, c3, *refs):
    edged = 1 in halves
    top, bottom = refs[:2] if edged else (None, None)
    refs = refs[2 * edged :]
    w_ref, shifted = refs[0], refs[-1]
    lay_shifted((c0, c1, c2, c3), top, bottom, rows, shifted)
    for i, half in enumerate(halves):
        own, following, send = refs[1 + 3 * i : 4 + 3 * i]
        for n in range(2):
            part = None
            for a in range(3):
                places = [rows.index(h - 1 + a) for h in ROWS[half][2 * n : 2 * n + 2]]
                source = jnp.concatenate([shifted[:, j * LANES : (j + 1) * LANES] for j in places], axis=1)
                term = jnp.dot(w_ref[a], source, preferred_element_type=F32)
                part = term if part is None else part + term
            lanes = slice(n * 256, (n + 1) * 256)
            own[0, :, lanes] = part[0:64]
            pair = (following.at[0], send.at[0, 0]) if half else (send.at[0, 0], following.at[0])
            pair[0][:, lanes] = part[64:128]
            pair[1][:, lanes] = part[128:192]
            send[1, 0, :, lanes] = part[192:256]


def conv(halves, at, chunks, sides, weights):
    rows = {(0,): (0, 1, 2, 3, 4, 5), (1,): (4, 5, 6, 7, 8, -1, 0, 1)}.get(halves, tuple(range(-1, 9)))
    single = jax.ShapeDtypeStruct((4, 64, 512), F32)
    double = jax.ShapeDtypeStruct((2, 4, 64, 512), F32)
    chunk = pl.BlockSpec((1, 64, 1024), lambda q: (q, 0, 0))
    edge = pl.BlockSpec((4, 1, 64, LANES), lambda q: (0, q, 0, 0))
    one = pl.BlockSpec((1, 64, 512), lambda q: (q, 0, 0))
    two = pl.BlockSpec((2, 1, 64, 512), lambda q: (0, q, 0, 0))
    sides = sides if 1 in halves else ()
    return pl.pallas_call(
        functools.partial(conv_kernel, halves, rows),
        out_shape=(single, single, double) * len(halves),
        grid=(4,),
        in_specs=[pl.BlockSpec(memory_space=pltpu.SMEM)]
        + [chunk] * 4
        + [edge] * len(sides)
        + [pl.BlockSpec((3, 256, 768), lambda q: (0, 0, 0))],
        out_specs=[one, one, two] * len(halves),
        scratch_shapes=[pltpu.VMEM((768, len(rows) * LANES), BF16)],
        compiler_params=params(16),
        cost_estimate=pl.CostEstimate(
            flops=2415919104 * len(halves), bytes_accessed=6000000 * len(halves), transcendentals=0
        ),
    )(at, *chunks, *sides, weights)


def kernel_grad_kernel(at, x0, x1, x2, x3, top, bottom, g0, g1, g2, g3, mine, other, shifted, grads, total):
    z, core, x, y = at[0], at[1], at[2], at[3]
    q = pl.program_id(0)
    lay_shifted((x0, x1, x2, x3), top, bottom, range(-1, 9), shifted)
    for k, g_ref in enumerate((g0, g1, g2, g3)):
        grads[k * 64 : (k + 1) * 64, :] = g_ref[0]

    @pl.when(q == 0)
    def _():
        total[...] = jnp.zeros_like(total)

    for a in range(3):
        total[a] += lax.dot_general(
            grads[...],
            shifted[:, a * LANES : a * LANES + 1024],
            (((1,), (1,)), ((), ())),
            preferred_element_type=F32,
        )

    @pl.when(q == 3)
    def _():
        for half, o_ref in ((core, mine), (1 - core, other)):
            second = jnp.where(half == y // 2, 0, 1)
            straight = second == lax.rem(y, 2)
            for k in range(4):
                member = lax.rem(z + (0, 1, 3, 2)[k], 4)
                rows = pl.ds(pl.multiple_of(place_of(member, x) * 64, 64), 64)
                for a in range(3):
                    for c in range(3):
                        lanes = pl.ds(pl.multiple_of(c * 256 + second * LANES, LANES), LANES)
                        tile = total[a, rows, lanes]
                        o_ref[k, a * 3 + c] = jnp.where(straight, tile, pltpu.roll(tile, W, 1))


def weight_grads(at, chunks, top, bottom, grads):
    shape = jax.ShapeDtypeStruct((4, 9, 64, LANES), F32)
    chunk = pl.BlockSpec((1, 64, 1024), lambda q: (q, 0, 0))
    edge = pl.BlockSpec((4, 1, 64, LANES), lambda q: (0, q, 0, 0))
    whole = pl.BlockSpec((4, 9, 64, LANES), lambda q: (0, 0, 0, 0))
    return pl.pallas_call(
        kernel_grad_kernel,
        out_shape=(shape,) * 2,
        grid=(4,),
        in_specs=[pl.BlockSpec(memory_space=pltpu.SMEM)] + [chunk] * 4 + [edge] * 2 + [chunk] * 4,
        out_specs=[whole] * 2,
        scratch_shapes=[
            pltpu.VMEM((768, 1280), BF16),
            pltpu.VMEM((256, 1024), BF16),
            pltpu.VMEM((3, 256, 768), F32),
        ],
        compiler_params=params(20),
        cost_estimate=pl.CostEstimate(flops=4831838208, bytes_accessed=9000000, transcendentals=0),
        name="weight_grads",
    )(at, *chunks, top, bottom, *grads)


def ring(step):
    return [(i, (i + step) % 4) for i in range(4)]


def after(value, *others):
    return lax.optimization_barrier((value, *others))[0]


def gather(block, axis):
    return (
        block, lax.ppermute(block, axis, FIRST), lax.ppermute(block, axis, SECOND), lax.ppermute(block, axis, OPPOSITE)
    )


def edges(chunks):
    forward = [(i, i + 1) for i in range(7)]
    backward = [(j, i) for i, j in forward]
    last = jnp.stack([chunk[:, :, -LANES:] for chunk in chunks])
    first = jnp.stack([chunk[:, :, :LANES] for chunk in chunks])
    return (lax.ppermute(last, ("z", "core"), forward), lax.ppermute(first, ("z", "core"), backward))


def reduce_second(a, b, one_a, one_b, axis):
    two_a = lax.ppermute(a[1] + one_a[1], axis, SECOND)
    two_b = lax.ppermute(b[1] + one_b[1], axis, FIRST)
    return a[0], one_a, two_a, b[0], one_b, two_b


def fetch_weights(at, block):
    along_z = gather(block, "z")
    own, first, second, far = route_weights(at, along_z)
    got = (own, lax.ppermute(first, "x", FIRST), lax.ppermute(second, "x", SECOND), lax.ppermute(far, "x", OPPOSITE))
    got = jnp.stack(got)
    return arrange_weights(at, got, lax.ppermute(got, "core", SWAP))


def step(images, kernel, upstream):
    at = jnp.stack([lax.axis_index(n) for n in ("z", "core", "x", "y")]).astype(jnp.int32)
    weights, turned = fetch_weights(at, kernel.reshape(9, 64, LANES))
    x, g = pack(images, upstream)
    x_chunks = gather(x, "y")
    g_chunks = gather(g, "x")

    x_sides = edges(x_chunks)
    g_sides = edges(g_chunks)
    out = conv((0, 1), at, x_chunks, x_sides, weights)
    out_a, out_b = out[:3], out[3:]
    out_one_a = lax.ppermute(out_a[2], "x", FIRST)
    out_one_b = lax.ppermute(out_b[2], "x", SECOND)
    grad = conv((0, 1), after(at, out_a[0]), g_chunks, g_sides, turned)
    grad_a, grad_b = grad[:3], grad[3:]
    grad_one_a = lax.ppermute(grad_a[2], "y", FIRST)
    grad_one_b = lax.ppermute(grad_b[2], "y", SECOND)

    near, far = weight_grads(after(at, grad_b[0]), x_chunks, *x_sides, g_chunks)
    near = near + lax.ppermute(far, "core", SWAP)
    output_maps = finish(*reduce_second(out_a, out_b, out_one_a, out_one_b, "x"))
    grad_pieces = reduce_second(grad_a, grad_b, grad_one_a, grad_one_b, "y")
    total = near[0]
    for k, turn in ((1, 1), (2, 3), (3, 2)):
        total = total + lax.ppermute(near[k], "z", ring(turn))
    cross = [(z * 4 + x, x * 4 + z) for z in range(4) for x in range(4)]
    home = lax.ppermute(total, ("z", "x"), cross)
    input_grad, kernel_grad = finish(*grad_pieces, home)
    return output_maps, input_grad, kernel_grad.reshape(3, 3, 64, LANES)


def solution(mesh):
    fine = Mesh(mesh.devices.reshape(4, 2, 4, 4), ("z", "core", "x", "y"))
    row, col = ("z", "core"), ("x", "y")
    flat = P(None, row, col)
    taps = P(None, None, col, row)
    return jax.shard_map(step, mesh=fine, in_specs=(flat, taps, flat), out_specs=(flat, flat, taps), check_vma=False)
```

```python
import functools

import jax
import jax.numpy as jnp
from jax import lax
from jax.experimental import pallas as pl
from jax.experimental.pallas import tpu as pltpu
from jax.sharding import Mesh, PartitionSpec as P


W = 64
LANES = 128
F32 = jnp.float32
BF16 = jnp.bfloat16

FIRST = [(0, 1), (1, 0), (2, 3), (3, 2)]
SECOND = [(1, 2), (2, 1), (3, 0), (0, 3)]
OPPOSITE = [(i, (i + 2) % 4) for i in range(4)]
SWAP = [(0, 1), (1, 0)]


def params(mib):
    return pltpu.CompilerParams(vmem_limit_bytes=mib * 1024 * 1024)


def lane_of(shape):
    return lax.broadcasted_iota(jnp.int32, shape, len(shape) - 1)


def row_of(shape):
    return lax.broadcasted_iota(jnp.int32, shape, len(shape) - 2)


def place_of(member, position):
    odd = lax.rem(position, 2)
    apart = lax.rem(member - position + 4, 4)
    return jnp.where(apart == 0, 0, jnp.where(apart == 2, 3, jnp.where(apart == 1, 1 + odd, 2 - odd)))


def pack_kernel(x_ref, g_ref, x_out, g_out, rows_ref, mix_ref):
    low = lane_of((32, LANES)) < W
    for i, (t, q) in enumerate((t, q) for t in range(2) for q in range(4)):
        b = i % 2
        source, target = ((x_ref, x_out), (g_ref, g_out))[t]
        for side in range(2):
            flat = source[q + 4 * side].astype(F32)
            for p in range(32):
                rows_ref[b, side, :, p, :] = flat[:, p * LANES : (p + 1) * LANES]
        for h in range(8):
            first = rows_ref[b, 0, h]
            second = rows_ref[b, 1, h]
            mix_ref[b, h, pl.ds(0, 32, stride=2), :] = jnp.where(low, first, pltpu.roll(second, W, 1))
            mix_ref[b, h, pl.ds(1, 32, stride=2), :] = jnp.where(low, pltpu.roll(first, W, 1), second)
        for h in range(8):
            target[q, :, h * LANES : (h + 1) * LANES] = mix_ref[b, h].astype(BF16)


def pack(x, g):
    shape = jax.ShapeDtypeStruct((4, 64, 1024), BF16)
    near = pl.BlockSpec(memory_space=pltpu.VMEM)
    return pl.pallas_call(
        pack_kernel,
        out_shape=(shape, shape),
        in_specs=[near] * 2,
        out_specs=[near] * 2,
        scratch_shapes=[pltpu.VMEM((2, 2, 8, 32, LANES), F32), pltpu.VMEM((2, 8, 64, LANES), F32)],
        compiler_params=params(8),
        name="pack",
    )(x, g)


ROWS = ((1, 2, 3, 4), (5, 6, 7, 0))


def finish_kernel(own_a, one_a, two_a, own_b, one_b, two_b, *refs):
    given, mix_ref, rows_ref, out_sem, more_sem = refs[-5:]
    o_hbm = refs[-6] if len(refs) == 6 else refs[1]
    more = pltpu.make_async_copy(refs[0], refs[2], more_sem) if len(refs) == 8 else None
    if more is not None:
        more.start()
    low = lane_of((32, LANES)) < W
    pieces = ((own_a, one_a, two_a), (own_b, one_b, two_b))

    def put(q, side):
        return pltpu.make_async_copy(given.at[q, side], o_hbm.at[q + 4 * side], out_sem.at[q, side])

    for q in range(4):
        b = q % 2
        for (own, one, two), rows in zip(pieces, ROWS):
            for j, h in enumerate(rows):
                lanes = slice(j * LANES, (j + 1) * LANES)
                mix_ref[b, h] = own[q, :, lanes] + one[0, q, :, lanes] + two[q, :, lanes]
        for h in range(8):
            even = mix_ref[b, h, pl.ds(0, 32, stride=2), :]
            odd = mix_ref[b, h, pl.ds(1, 32, stride=2), :]
            rows_ref[b, 0, h] = jnp.where(low, even, pltpu.roll(odd, W, 1))
            rows_ref[b, 1, h] = jnp.where(low, pltpu.roll(even, W, 1), odd)
        for side in range(2):
            for p in range(32):
                given[q, side, :, p * LANES : (p + 1) * LANES] = rows_ref[b, side, :, p, :].astype(BF16)
            put(q, side).start()
    for q in range(4):
        for side in range(2):
            put(q, side).wait()
    if more is not None:
        more.wait()


def finish(*pieces):
    shapes = [jax.ShapeDtypeStruct((8, 8, 4096), BF16)]
    shapes += [jax.ShapeDtypeStruct(piece.shape, piece.dtype) for piece in pieces[6:]]
    specs = [pl.BlockSpec(memory_space=pl.ANY)] * len(shapes)
    return pl.pallas_call(
        finish_kernel,
        out_shape=shapes if len(shapes) > 1 else shapes[0],
        in_specs=[pl.BlockSpec(memory_space=pltpu.VMEM)] * len(pieces),
        out_specs=specs if len(shapes) > 1 else specs[0],
        scratch_shapes=[
            pltpu.VMEM((4, 2, 8, 4096), BF16),
            pltpu.VMEM((2, 8, 64, LANES), F32),
            pltpu.VMEM((2, 2, 8, 32, LANES), F32),
            pltpu.SemaphoreType.DMA((4, 2)),
            pltpu.SemaphoreType.DMA,
        ],
        compiler_params=params(12),
        name="finish",
    )(*pieces)


def listed(position, k):
    odd = lax.rem(position, 2)
    return lax.rem(position + (0, 1 + 2 * odd, 3 - 2 * odd, 2)[k], 4)


def route_kernel(at, b0, b1, b2, b3, o0, o1, o2, o3, held):
    for k, ref in enumerate((b0, b1, b2, b3)):
        held[k] = ref[...]
    for k, ref in enumerate((o0, o1, o2, o3)):
        ref[...] = held[place_of(listed(at[2], k), at[0])]


def route_weights(at, blocks):
    shape = jax.ShapeDtypeStruct((9, 64, LANES), BF16)
    near = pl.BlockSpec(memory_space=pltpu.VMEM)
    return pl.pallas_call(
        route_kernel,
        out_shape=(shape,) * 4,
        in_specs=[pl.BlockSpec(memory_space=pltpu.SMEM)] + [near] * 4,
        out_specs=[near] * 4,
        scratch_shapes=[pltpu.VMEM((4, 9, 64, LANES), BF16)],
        compiler_params=params(4),
        name="route",
    )(at, *blocks)


def weights_kernel(at, mine, other, w_ref, wt_ref, whole):
    core, y = at[1], at[3]
    for ref, side in ((mine, core), (other, 1 - core)):
        lanes = pl.ds(pl.multiple_of(side * LANES, LANES), LANES)
        for k in range(4):
            for tap in range(9):
                whole[tap, k * 64 : (k + 1) * 64, lanes] = ref[k, tap]
    place, channel = row_of((256, 256)), lane_of((256, 256))
    order = jnp.where(
        (place_of(channel // 64, y) == place // 64) & (channel % 64 == place % 64), 1.0, 0.0
    ).astype(BF16)
    across = (((1,), (1,)), ((), ()))
    for tap in range(9):
        straight = lax.dot_general(whole[tap], order, across, preferred_element_type=F32).astype(BF16)
        turned = lax.dot_general(order, whole[tap], across, preferred_element_type=F32).astype(BF16)
        a, c = tap // 3, tap % 3
        w_ref[a, :, c * 256 : (c + 1) * 256] = straight
        wt_ref[2 - a, :, (2 - c) * 256 : (3 - c) * 256] = turned


def arrange_weights(at, mine, other):
    shape = jax.ShapeDtypeStruct((3, 256, 768), BF16)
    return pl.pallas_call(
        weights_kernel,
        out_shape=(shape, shape),
        in_specs=[pl.BlockSpec(memory_space=pltpu.SMEM)] + [pl.BlockSpec(memory_space=pltpu.VMEM)] * 2,
        out_specs=[pl.BlockSpec(memory_space=pltpu.VMEM)] * 2,
        scratch_shapes=[pltpu.VMEM((9, 256, 256), BF16)],
        compiler_params=params(20),
        name="weights",
    )(at, mine, other)


def lay_shifted(q, chunks, top, bottom, rows, shifted):
    column = lane_of((64, LANES)) % W
    not_first = jnp.where(column == 0, 0.0, 1.0).astype(BF16)
    not_last = jnp.where(column == W - 1, 0.0, 1.0).astype(BF16)
    for k in range(4):
        at = k * 64
        for j, h in enumerate(rows):
            if h == -1:
                tile = top[k, q]
            elif h == 8:
                tile = bottom[k, q]
            else:
                tile = chunks[k][q, :, h * LANES : (h + 1) * LANES]
            lanes = slice(j * LANES, (j + 1) * LANES)
            shifted[at : at + 64, lanes] = pltpu.roll(tile, 1, 1) * not_first
            shifted[256 + at : 320 + at, lanes] = tile
            shifted[512 + at : 576 + at, lanes] = pltpu.roll(tile, LANES - 1, 1) * not_last


def conv_kernel(halves, rows, at, c0, c1, c2, c3, *refs):
    edged = 1 in halves
    top, bottom = refs[:2] if edged else (None, None)
    refs = refs[2 * edged :]
    w_ref, both = refs[0], refs[-1]

    def lay(q, shifted):
        lay_shifted(q, (c0, c1, c2, c3), top, bottom, rows, shifted)

    def multiply(q, shifted):
        for i, half in enumerate(halves):
            own, following, send = refs[1 + 3 * i : 4 + 3 * i]
            for n in range(2):
                part = None
                for a in range(3):
                    places = [rows.index(h - 1 + a) for h in ROWS[half][2 * n : 2 * n + 2]]
                    source = jnp.concatenate([shifted[:, j * LANES : (j + 1) * LANES] for j in places], axis=1)
                    term = jnp.dot(w_ref[a], source, preferred_element_type=F32)
                    part = term if part is None else part + term
                lanes = slice(n * 256, (n + 1) * 256)
                own[q, :, lanes] = part[0:64]
                pair = (following.at[q], send.at[0, q]) if half else (send.at[0, q], following.at[q])
                pair[0][:, lanes] = part[64:128]
                pair[1][:, lanes] = part[128:192]
                send[1, q, :, lanes] = part[192:256]

    lay(0, both.at[0])
    for q in range(4):
        if q < 3:
            lay(q + 1, both.at[(q + 1) % 2])
        multiply(q, both.at[q % 2])


def conv(halves, at, chunks, sides, weights):
    rows = {(0,): (0, 1, 2, 3, 4, 5), (1,): (4, 5, 6, 7, 8, -1, 0, 1)}.get(halves, tuple(range(-1, 9)))
    single = jax.ShapeDtypeStruct((4, 64, 512), F32)
    double = jax.ShapeDtypeStruct((2, 4, 64, 512), F32)
    near = pl.BlockSpec(memory_space=pltpu.VMEM)
    sides = sides if 1 in halves else ()
    return pl.pallas_call(
        functools.partial(conv_kernel, halves, rows),
        out_shape=(single, single, double) * len(halves),
        in_specs=[pl.BlockSpec(memory_space=pltpu.SMEM)] + [near] * (5 + len(sides)),
        out_specs=[near] * (3 * len(halves)),
        scratch_shapes=[pltpu.VMEM((2, 768, len(rows) * LANES), BF16)],
        compiler_params=params(20),
        cost_estimate=pl.CostEstimate(
            flops=2415919104 * len(halves), bytes_accessed=6000000 * len(halves), transcendentals=0
        ),
    )(at, *chunks, *sides, weights)


def kernel_grad_kernel(at, x0, x1, x2, x3, top, bottom, g0, g1, g2, g3, mine, other, shifted, grads, total):
    z, core, x, y = at[0], at[1], at[2], at[3]

    def add(q, first):
        lay_shifted(q, (x0, x1, x2, x3), top, bottom, range(-1, 9), shifted)
        for k, g_ref in enumerate((g0, g1, g2, g3)):
            grads[k * 64 : (k + 1) * 64, :] = g_ref[q]
        for a in range(3):
            term = lax.dot_general(
                grads[...],
                shifted[:, a * LANES : a * LANES + 1024],
                (((1,), (1,)), ((), ())),
                preferred_element_type=F32,
            )
            total[a] = term if first else total[a] + term

    add(0, True)

    @pl.loop(1, 4)
    def _(q):
        add(q, False)

    for half, o_ref in ((core, mine), (1 - core, other)):
        second = jnp.where(half == y // 2, 0, 1)
        straight = second == lax.rem(y, 2)
        for k in range(4):
            member = lax.rem(z + (0, 1, 3, 2)[k], 4)
            rows = pl.ds(pl.multiple_of(place_of(member, x) * 64, 64), 64)
            for a in range(3):
                for c in range(3):
                    lanes = pl.ds(pl.multiple_of(c * 256 + second * LANES, LANES), LANES)
                    tile = total[a, rows, lanes]
                    o_ref[k, a * 3 + c] = jnp.where(straight, tile, pltpu.roll(tile, W, 1))


def weight_grads(at, chunks, top, bottom, grads):
    shape = jax.ShapeDtypeStruct((4, 9, 64, LANES), F32)
    near = pl.BlockSpec(memory_space=pltpu.VMEM)
    return pl.pallas_call(
        kernel_grad_kernel,
        out_shape=(shape,) * 2,
        in_specs=[pl.BlockSpec(memory_space=pltpu.SMEM)] + [near] * 10,
        out_specs=[near] * 2,
        scratch_shapes=[pltpu.VMEM((768, 1280), BF16), pltpu.VMEM((256, 1024), BF16), pltpu.VMEM((3, 256, 768), F32)],
        compiler_params=params(20),
        cost_estimate=pl.CostEstimate(flops=4831838208, bytes_accessed=9000000, transcendentals=0),
        name="weight_grads",
    )(at, *chunks, top, bottom, *grads)


def ring(step):
    return [(i, (i + step) % 4) for i in range(4)]


def after(value, *others):
    return lax.optimization_barrier((value, *others))[0]


def gather(block, axis):
    return (
        block, lax.ppermute(block, axis, FIRST), lax.ppermute(block, axis, SECOND), lax.ppermute(block, axis, OPPOSITE)
    )


def edges(chunks):
    forward = [(i, i + 1) for i in range(7)]
    backward = [(j, i) for i, j in forward]
    last = jnp.stack([chunk[:, :, -LANES:] for chunk in chunks])
    first = jnp.stack([chunk[:, :, :LANES] for chunk in chunks])
    return (lax.ppermute(last, ("z", "core"), forward), lax.ppermute(first, ("z", "core"), backward))


def reduce_second(a, b, one_a, one_b, axis):
    two_a = lax.ppermute(a[1] + one_a[1], axis, SECOND)
    two_b = lax.ppermute(b[1] + one_b[1], axis, FIRST)
    return a[0], one_a, two_a, b[0], one_b, two_b


def fetch_weights(at, block):
    along_z = gather(block, "z")
    own, first, second, far = route_weights(at, along_z)
    got = (own, lax.ppermute(first, "x", FIRST), lax.ppermute(second, "x", SECOND), lax.ppermute(far, "x", OPPOSITE))
    got = jnp.stack(got)
    return arrange_weights(at, got, lax.ppermute(got, "core", SWAP))


def step(images, kernel, upstream):
    at = jnp.stack([lax.axis_index(n) for n in ("z", "core", "x", "y")]).astype(jnp.int32)
    weights, turned = fetch_weights(at, kernel.reshape(9, 64, LANES))
    x, g = pack(images, upstream)
    x_chunks = gather(x, "y")
    g_chunks = gather(g, "x")

    x_sides = edges(x_chunks)
    g_sides = edges(g_chunks)
    out = conv((0, 1), at, x_chunks, x_sides, weights)
    out_a, out_b = out[:3], out[3:]
    out_one_a = lax.ppermute(out_a[2], "x", FIRST)
    out_one_b = lax.ppermute(out_b[2], "x", SECOND)
    grad_a = conv((0,), after(at, out_a[0]), g_chunks, g_sides, turned)
    grad_one_a = lax.ppermute(grad_a[2], "y", FIRST)
    grad_b = conv((1,), after(at, grad_a[0]), g_chunks, g_sides, turned)
    grad_one_b = lax.ppermute(grad_b[2], "y", SECOND)

    near, far = weight_grads(after(at, grad_b[0]), x_chunks, *x_sides, g_chunks)
    near = near + lax.ppermute(far, "core", SWAP)
    output_maps = finish(*reduce_second(out_a, out_b, out_one_a, out_one_b, "x"))
    grad_pieces = reduce_second(grad_a, grad_b, grad_one_a, grad_one_b, "y")
    total = near[0]
    for k, turn in ((1, 1), (2, 3), (3, 2)):
        total = total + lax.ppermute(near[k], "z", ring(turn))
    cross = [(z * 4 + x, x * 4 + z) for z in range(4) for x in range(4)]
    home = lax.ppermute(total, ("z", "x"), cross)
    input_grad, kernel_grad = finish(*grad_pieces, home)
    return output_maps, input_grad, kernel_grad.reshape(3, 3, 64, LANES)


def solution(mesh):
    fine = Mesh(mesh.devices.reshape(4, 2, 4, 4), ("z", "core", "x", "y"))
    row, col = ("z", "core"), ("x", "y")
    flat = P(None, row, col)
    taps = P(None, None, col, row)
    return jax.shard_map(step, mesh=fine, in_specs=(flat, taps, flat), out_specs=(flat, flat, taps), check_vma=False)
```

```python
import functools

import jax
import jax.numpy as jnp
from jax import lax
from jax.experimental import pallas as pl
from jax.experimental.pallas import tpu as pltpu
from jax.sharding import Mesh, PartitionSpec as P


W = 64
LANES = 128
F32 = jnp.float32
BF16 = jnp.bfloat16

FIRST = [(0, 1), (1, 0), (2, 3), (3, 2)]
SECOND = [(1, 2), (2, 1), (3, 0), (0, 3)]
OPPOSITE = [(i, (i + 2) % 4) for i in range(4)]
SWAP = [(0, 1), (1, 0)]


def params(mib):
    return pltpu.CompilerParams(vmem_limit_bytes=mib * 1024 * 1024)


def lane_of(shape):
    return lax.broadcasted_iota(jnp.int32, shape, len(shape) - 1)


def row_of(shape):
    return lax.broadcasted_iota(jnp.int32, shape, len(shape) - 2)


def place_of(member, position):
    odd = lax.rem(position, 2)
    apart = lax.rem(member - position + 4, 4)
    return jnp.where(apart == 0, 0, jnp.where(apart == 2, 3, jnp.where(apart == 1, 1 + odd, 2 - odd)))


def pack_kernel(x_hbm, g_hbm, x_out, g_out, taken, rows_ref, mix_ref, in_sem):
    low = lane_of((32, LANES)) < W
    pieces = [(t, q) for t in range(2) for q in range(4)]

    def fetch(t, q, side):
        source = (x_hbm, g_hbm)[t].at[q + 4 * side]
        return pltpu.make_async_copy(source, taken.at[t, q, side], in_sem.at[t, q, side])

    for t, q in pieces:
        for side in range(2):
            fetch(t, q, side).start()
    for i, (t, q) in enumerate(pieces):
        b = i % 2
        target = (x_out, g_out)[t]
        for side in range(2):
            fetch(t, q, side).wait()
        for side in range(2):
            flat = taken[t, q, side].astype(F32)
            for p in range(32):
                rows_ref[b, side, :, p, :] = flat[:, p * LANES : (p + 1) * LANES]
        for h in range(8):
            first = rows_ref[b, 0, h]
            second = rows_ref[b, 1, h]
            mix_ref[b, h, pl.ds(0, 32, stride=2), :] = jnp.where(low, first, pltpu.roll(second, W, 1))
            mix_ref[b, h, pl.ds(1, 32, stride=2), :] = jnp.where(low, pltpu.roll(first, W, 1), second)
        for h in range(8):
            target[q, :, h * LANES : (h + 1) * LANES] = mix_ref[b, h].astype(BF16)


def pack(x, g):
    shape = jax.ShapeDtypeStruct((4, 64, 1024), BF16)
    far = pl.BlockSpec(memory_space=pltpu.HBM)
    near = pl.BlockSpec(memory_space=pltpu.VMEM)
    return pl.pallas_call(
        pack_kernel,
        out_shape=(shape, shape),
        in_specs=[far] * 2,
        out_specs=[near] * 2,
        scratch_shapes=[
            pltpu.VMEM((2, 4, 2, 8, 4096), BF16),
            pltpu.VMEM((2, 2, 8, 32, LANES), F32),
            pltpu.VMEM((2, 8, 64, LANES), F32),
            pltpu.SemaphoreType.DMA((2, 4, 2)),
        ],
        compiler_params=params(8),
        name="pack",
    )(*(pltpu.with_memory_space_constraint(a, pltpu.HBM) for a in (x, g)))


ROWS = ((1, 2, 3, 4), (5, 6, 7, 0))


def finish_kernel(own_a, one_a, two_a, own_b, one_b, two_b, *refs):
    given, mix_ref, rows_ref, out_sem, more_sem = refs[-5:]
    o_hbm = refs[-6] if len(refs) == 6 else refs[1]
    more = pltpu.make_async_copy(refs[0], refs[2], more_sem) if len(refs) == 8 else None
    if more is not None:
        more.start()
    low = lane_of((32, LANES)) < W
    pieces = ((own_a, one_a, two_a), (own_b, one_b, two_b))

    def put(q, side):
        return pltpu.make_async_copy(given.at[q, side], o_hbm.at[q + 4 * side], out_sem.at[q, side])

    for q in range(4):
        b = q % 2
        for (own, one, two), rows in zip(pieces, ROWS):
            for j, h in enumerate(rows):
                lanes = slice(j * LANES, (j + 1) * LANES)
                mix_ref[b, h] = own[q, :, lanes] + one[0, q, :, lanes] + two[q, :, lanes]
        for h in range(8):
            even = mix_ref[b, h, pl.ds(0, 32, stride=2), :]
            odd = mix_ref[b, h, pl.ds(1, 32, stride=2), :]
            rows_ref[b, 0, h] = jnp.where(low, even, pltpu.roll(odd, W, 1))
            rows_ref[b, 1, h] = jnp.where(low, pltpu.roll(even, W, 1), odd)
        for side in range(2):
            for p in range(32):
                given[q, side, :, p * LANES : (p + 1) * LANES] = rows_ref[b, side, :, p, :].astype(BF16)
            put(q, side).start()
    for q in range(4):
        for side in range(2):
            put(q, side).wait()
    if more is not None:
        more.wait()


def finish(*pieces):
    shapes = [jax.ShapeDtypeStruct((8, 8, 4096), BF16)]
    shapes += [jax.ShapeDtypeStruct(piece.shape, piece.dtype) for piece in pieces[6:]]
    specs = [pl.BlockSpec(memory_space=pl.ANY)] * len(shapes)
    return pl.pallas_call(
        finish_kernel,
        out_shape=shapes if len(shapes) > 1 else shapes[0],
        in_specs=[pl.BlockSpec(memory_space=pltpu.VMEM)] * len(pieces),
        out_specs=specs if len(shapes) > 1 else specs[0],
        scratch_shapes=[
            pltpu.VMEM((4, 2, 8, 4096), BF16),
            pltpu.VMEM((2, 8, 64, LANES), F32),
            pltpu.VMEM((2, 2, 8, 32, LANES), F32),
            pltpu.SemaphoreType.DMA((4, 2)),
            pltpu.SemaphoreType.DMA,
        ],
        compiler_params=params(12),
        name="finish",
    )(*pieces)


def listed(position, k):
    odd = lax.rem(position, 2)
    return lax.rem(position + (0, 1 + 2 * odd, 3 - 2 * odd, 2)[k], 4)


def route_kernel(at, b0, b1, b2, b3, o0, o1, o2, o3, held):
    for k, ref in enumerate((b0, b1, b2, b3)):
        held[k] = ref[...]
    for k, ref in enumerate((o0, o1, o2, o3)):
        ref[...] = held[place_of(listed(at[2], k), at[0])]


def route_weights(at, blocks):
    shape = jax.ShapeDtypeStruct((9, 64, LANES), BF16)
    near = pl.BlockSpec(memory_space=pltpu.VMEM)
    return pl.pallas_call(
        route_kernel,
        out_shape=(shape,) * 4,
        in_specs=[pl.BlockSpec(memory_space=pltpu.SMEM)] + [near] * 4,
        out_specs=[near] * 4,
        scratch_shapes=[pltpu.VMEM((4, 9, 64, LANES), BF16)],
        compiler_params=params(4),
        name="route",
    )(at, *blocks)


def weights_kernel(at, mine, other, w_ref, wt_ref, whole):
    core, y = at[1], at[3]
    for ref, side in ((mine, core), (other, 1 - core)):
        lanes = pl.ds(pl.multiple_of(side * LANES, LANES), LANES)
        for k in range(4):
            for tap in range(9):
                whole[tap, k * 64 : (k + 1) * 64, lanes] = ref[k, tap]
    place, channel = row_of((256, 256)), lane_of((256, 256))
    order = jnp.where(
        (place_of(channel // 64, y) == place // 64) & (channel % 64 == place % 64), 1.0, 0.0
    ).astype(BF16)
    across = (((1,), (1,)), ((), ()))
    for tap in range(9):
        straight = lax.dot_general(whole[tap], order, across, preferred_element_type=F32).astype(BF16)
        turned = lax.dot_general(order, whole[tap], across, preferred_element_type=F32).astype(BF16)
        a, c = tap // 3, tap % 3
        w_ref[a, :, c * 256 : (c + 1) * 256] = straight
        wt_ref[2 - a, :, (2 - c) * 256 : (3 - c) * 256] = turned


def arrange_weights(at, mine, other):
    shape = jax.ShapeDtypeStruct((3, 256, 768), BF16)
    return pl.pallas_call(
        weights_kernel,
        out_shape=(shape, shape),
        in_specs=[pl.BlockSpec(memory_space=pltpu.SMEM)] + [pl.BlockSpec(memory_space=pltpu.VMEM)] * 2,
        out_specs=[pl.BlockSpec(memory_space=pltpu.VMEM)] * 2,
        scratch_shapes=[pltpu.VMEM((9, 256, 256), BF16)],
        compiler_params=params(20),
        name="weights",
    )(at, mine, other)


def lay_shifted(q, chunks, top, bottom, rows, shifted):
    column = lane_of((64, LANES)) % W
    not_first = jnp.where(column == 0, 0.0, 1.0).astype(BF16)
    not_last = jnp.where(column == W - 1, 0.0, 1.0).astype(BF16)
    for k in range(4):
        at = k * 64
        for j, h in enumerate(rows):
            if h == -1:
                tile = top[k, q]
            elif h == 8:
                tile = bottom[k, q]
            else:
                tile = chunks[k][q, :, h * LANES : (h + 1) * LANES]
            lanes = slice(j * LANES, (j + 1) * LANES)
            shifted[at : at + 64, lanes] = pltpu.roll(tile, 1, 1) * not_first
            shifted[256 + at : 320 + at, lanes] = tile
            shifted[512 + at : 576 + at, lanes] = pltpu.roll(tile, LANES - 1, 1) * not_last


def conv_kernel(halves, rows, at, c0, c1, c2, c3, *refs):
    edged = 1 in halves
    top, bottom = refs[:2] if edged else (None, None)
    refs = refs[2 * edged :]
    w_ref, both = refs[0], refs[-1]

    def lay(q, shifted):
        lay_shifted(q, (c0, c1, c2, c3), top, bottom, rows, shifted)

    def multiply(q, shifted):
        for i, half in enumerate(halves):
            own, following, send = refs[1 + 3 * i : 4 + 3 * i]
            for n in range(2):
                part = None
                for a in range(3):
                    places = [rows.index(h - 1 + a) for h in ROWS[half][2 * n : 2 * n + 2]]
                    source = jnp.concatenate([shifted[:, j * LANES : (j + 1) * LANES] for j in places], axis=1)
                    term = jnp.dot(w_ref[a], source, preferred_element_type=F32)
                    part = term if part is None else part + term
                lanes = slice(n * 256, (n + 1) * 256)
                own[q, :, lanes] = part[0:64]
                pair = (following.at[q], send.at[0, q]) if half else (send.at[0, q], following.at[q])
                pair[0][:, lanes] = part[64:128]
                pair[1][:, lanes] = part[128:192]
                send[1, q, :, lanes] = part[192:256]

    lay(0, both.at[0])
    for q in range(4):
        if q < 3:
            lay(q + 1, both.at[(q + 1) % 2])
        multiply(q, both.at[q % 2])


def conv(halves, at, chunks, sides, weights):
    rows = {(0,): (0, 1, 2, 3, 4, 5), (1,): (4, 5, 6, 7, 8, -1, 0, 1)}.get(halves, tuple(range(-1, 9)))
    single = jax.ShapeDtypeStruct((4, 64, 512), F32)
    double = jax.ShapeDtypeStruct((2, 4, 64, 512), F32)
    near = pl.BlockSpec(memory_space=pltpu.VMEM)
    sides = sides if 1 in halves else ()
    return pl.pallas_call(
        functools.partial(conv_kernel, halves, rows),
        out_shape=(single, single, double) * len(halves),
        in_specs=[pl.BlockSpec(memory_space=pltpu.SMEM)] + [near] * (5 + len(sides)),
        out_specs=[near] * (3 * len(halves)),
        scratch_shapes=[pltpu.VMEM((2, 768, len(rows) * LANES), BF16)],
        compiler_params=params(20),
        cost_estimate=pl.CostEstimate(
            flops=2415919104 * len(halves), bytes_accessed=6000000 * len(halves), transcendentals=0
        ),
    )(at, *chunks, *sides, weights)


def kernel_grad_kernel(at, x0, x1, x2, x3, top, bottom, g0, g1, g2, g3, mine, other, shifted, grads, total):
    z, core, x, y = at[0], at[1], at[2], at[3]

    def add(q, first):
        lay_shifted(q, (x0, x1, x2, x3), top, bottom, range(-1, 9), shifted)
        for k, g_ref in enumerate((g0, g1, g2, g3)):
            grads[k * 64 : (k + 1) * 64, :] = g_ref[q]
        for a in range(3):
            term = lax.dot_general(
                grads[...],
                shifted[:, a * LANES : a * LANES + 1024],
                (((1,), (1,)), ((), ())),
                preferred_element_type=F32,
            )
            total[a] = term if first else total[a] + term

    add(0, True)

    @pl.loop(1, 4)
    def _(q):
        add(q, False)

    for half, o_ref in ((core, mine), (1 - core, other)):
        second = jnp.where(half == y // 2, 0, 1)
        straight = second == lax.rem(y, 2)
        for k in range(4):
            member = lax.rem(z + (0, 1, 3, 2)[k], 4)
            rows = pl.ds(pl.multiple_of(place_of(member, x) * 64, 64), 64)
            for a in range(3):
                for c in range(3):
                    lanes = pl.ds(pl.multiple_of(c * 256 + second * LANES, LANES), LANES)
                    tile = total[a, rows, lanes]
                    o_ref[k, a * 3 + c] = jnp.where(straight, tile, pltpu.roll(tile, W, 1))


def weight_grads(at, chunks, top, bottom, grads):
    shape = jax.ShapeDtypeStruct((4, 9, 64, LANES), F32)
    near = pl.BlockSpec(memory_space=pltpu.VMEM)
    return pl.pallas_call(
        kernel_grad_kernel,
        out_shape=(shape,) * 2,
        in_specs=[pl.BlockSpec(memory_space=pltpu.SMEM)] + [near] * 10,
        out_specs=[near] * 2,
        scratch_shapes=[pltpu.VMEM((768, 1280), BF16), pltpu.VMEM((256, 1024), BF16), pltpu.VMEM((3, 256, 768), F32)],
        compiler_params=params(20),
        cost_estimate=pl.CostEstimate(flops=4831838208, bytes_accessed=9000000, transcendentals=0),
        name="weight_grads",
    )(at, *chunks, top, bottom, *grads)


def ring(step):
    return [(i, (i + step) % 4) for i in range(4)]


def after(value, *others):
    return lax.optimization_barrier((value, *others))[0]


def gather(block, axis):
    return (
        block, lax.ppermute(block, axis, FIRST), lax.ppermute(block, axis, SECOND), lax.ppermute(block, axis, OPPOSITE)
    )


def edges(chunks):
    forward = [(i, i + 1) for i in range(7)]
    backward = [(j, i) for i, j in forward]
    last = jnp.stack([chunk[:, :, -LANES:] for chunk in chunks])
    first = jnp.stack([chunk[:, :, :LANES] for chunk in chunks])
    return (lax.ppermute(last, ("z", "core"), forward), lax.ppermute(first, ("z", "core"), backward))


def reduce_second(a, b, one_a, one_b, axis):
    two_a = lax.ppermute(a[1] + one_a[1], axis, SECOND)
    two_b = lax.ppermute(b[1] + one_b[1], axis, FIRST)
    return a[0], one_a, two_a, b[0], one_b, two_b


def fetch_weights(at, block):
    along_z = gather(block, "z")
    own, first, second, far = route_weights(at, along_z)
    got = (own, lax.ppermute(first, "x", FIRST), lax.ppermute(second, "x", SECOND), lax.ppermute(far, "x", OPPOSITE))
    got = jnp.stack(got)
    return arrange_weights(at, got, lax.ppermute(got, "core", SWAP))


def step(images, kernel, upstream):
    at = jnp.stack([lax.axis_index(n) for n in ("z", "core", "x", "y")]).astype(jnp.int32)
    weights, turned = fetch_weights(at, kernel.reshape(9, 64, LANES))
    x, g = pack(images, upstream)
    x_chunks = gather(x, "y")
    g_chunks = gather(g, "x")

    x_sides = edges(x_chunks)
    g_sides = edges(g_chunks)
    out = conv((0, 1), at, x_chunks, x_sides, weights)
    out_a, out_b = out[:3], out[3:]
    out_one_a = lax.ppermute(out_a[2], "x", FIRST)
    out_one_b = lax.ppermute(out_b[2], "x", SECOND)
    grad_a = conv((0,), after(at, out_a[0]), g_chunks, g_sides, turned)
    grad_one_a = lax.ppermute(grad_a[2], "y", FIRST)
    grad_b = conv((1,), after(at, grad_a[0]), g_chunks, g_sides, turned)
    grad_one_b = lax.ppermute(grad_b[2], "y", SECOND)

    near, far = weight_grads(after(at, grad_b[0]), x_chunks, *x_sides, g_chunks)
    near = near + lax.ppermute(far, "core", SWAP)
    output_maps = finish(*reduce_second(out_a, out_b, out_one_a, out_one_b, "x"))
    grad_pieces = reduce_second(grad_a, grad_b, grad_one_a, grad_one_b, "y")
    total = near[0]
    for k, turn in ((1, 1), (2, 3), (3, 2)):
        total = total + lax.ppermute(near[k], "z", ring(turn))
    cross = [(z * 4 + x, x * 4 + z) for z in range(4) for x in range(4)]
    home = lax.ppermute(total, ("z", "x"), cross)
    input_grad, kernel_grad = finish(*grad_pieces, home)
    return output_maps, input_grad, kernel_grad.reshape(3, 3, 64, LANES)


def solution(mesh):
    fine = Mesh(mesh.devices.reshape(4, 2, 4, 4), ("z", "core", "x", "y"))
    row, col = ("z", "core"), ("x", "y")
    flat = P(None, row, col)
    taps = P(None, None, col, row)
    return jax.shard_map(step, mesh=fine, in_specs=(flat, taps, flat), out_specs=(flat, flat, taps), check_vma=False)
```

```python
import functools

import jax
import jax.numpy as jnp
from jax import lax
from jax.experimental import pallas as pl
from jax.experimental.pallas import tpu as pltpu
from jax.sharding import Mesh, PartitionSpec as P


W = 64
LANES = 128
F32 = jnp.float32
BF16 = jnp.bfloat16

FIRST = [(0, 1), (1, 0), (2, 3), (3, 2)]
SECOND = [(1, 2), (2, 1), (3, 0), (0, 3)]
OPPOSITE = [(i, (i + 2) % 4) for i in range(4)]
SWAP = [(0, 1), (1, 0)]


def params(mib):
    return pltpu.CompilerParams(vmem_limit_bytes=mib * 1024 * 1024)


def lane_of(shape):
    return lax.broadcasted_iota(jnp.int32, shape, len(shape) - 1)


def row_of(shape):
    return lax.broadcasted_iota(jnp.int32, shape, len(shape) - 2)


def place_of(member, position):
    odd = lax.rem(position, 2)
    apart = lax.rem(member - position + 4, 4)
    return jnp.where(apart == 0, 0, jnp.where(apart == 2, 3, jnp.where(apart == 1, 1 + odd, 2 - odd)))


def pack_kernel(x_hbm, g_hbm, x_out, g_out, taken, rows_ref, mix_ref, in_sem):
    low = lane_of((32, LANES)) < W
    pieces = [(t, q) for t in range(2) for q in range(4)]

    def fetch(t, q, side):
        source = (x_hbm, g_hbm)[t].at[q + 4 * side]
        return pltpu.make_async_copy(source, taken.at[t, q, side], in_sem.at[t, q, side])

    for t, q in pieces:
        for side in range(2):
            fetch(t, q, side).start()
    for i, (t, q) in enumerate(pieces):
        b = i % 2
        target = (x_out, g_out)[t]
        for side in range(2):
            fetch(t, q, side).wait()
        for side in range(2):
            flat = taken[t, q, side].astype(F32)
            for p in range(32):
                rows_ref[b, side, :, p, :] = flat[:, p * LANES : (p + 1) * LANES]
        for h in range(8):
            first = rows_ref[b, 0, h]
            second = rows_ref[b, 1, h]
            mix_ref[b, h, pl.ds(0, 32, stride=2), :] = jnp.where(low, first, pltpu.roll(second, W, 1))
            mix_ref[b, h, pl.ds(1, 32, stride=2), :] = jnp.where(low, pltpu.roll(first, W, 1), second)
        for h in range(8):
            target[q, :, h * LANES : (h + 1) * LANES] = mix_ref[b, h].astype(BF16)


def pack(x, g):
    shape = jax.ShapeDtypeStruct((4, 64, 1024), BF16)
    far = pl.BlockSpec(memory_space=pltpu.HBM)
    near = pl.BlockSpec(memory_space=pltpu.VMEM)
    return pl.pallas_call(
        pack_kernel,
        out_shape=(shape, shape),
        in_specs=[far] * 2,
        out_specs=[near] * 2,
        scratch_shapes=[
            pltpu.VMEM((2, 4, 2, 8, 4096), BF16),
            pltpu.VMEM((2, 2, 8, 32, LANES), F32),
            pltpu.VMEM((2, 8, 64, LANES), F32),
            pltpu.SemaphoreType.DMA((2, 4, 2)),
        ],
        compiler_params=params(8),
        name="pack",
    )(*(pltpu.with_memory_space_constraint(a, pltpu.HBM) for a in (x, g)))


ROWS = ((1, 2, 3, 4), (5, 6, 7, 0))


def finish_kernel(own_a, one_a, two_a, own_b, one_b, two_b, *refs):
    given, mix_ref, rows_ref, out_sem, more_sem = refs[-5:]
    o_hbm = refs[-6] if len(refs) == 6 else refs[1]
    more = pltpu.make_async_copy(refs[0], refs[2], more_sem) if len(refs) == 8 else None
    if more is not None:
        more.start()
    low = lane_of((32, LANES)) < W
    pieces = ((own_a, one_a, two_a), (own_b, one_b, two_b))

    def put(q, side):
        return pltpu.make_async_copy(given.at[q, side], o_hbm.at[q + 4 * side], out_sem.at[q, side])

    for q in range(4):
        b = q % 2
        for (own, one, two), rows in zip(pieces, ROWS):
            for j, h in enumerate(rows):
                lanes = slice(j * LANES, (j + 1) * LANES)
                mix_ref[b, h] = own[q, :, lanes] + one[0, q, :, lanes] + two[q, :, lanes]
        for h in range(8):
            even = mix_ref[b, h, pl.ds(0, 32, stride=2), :]
            odd = mix_ref[b, h, pl.ds(1, 32, stride=2), :]
            rows_ref[b, 0, h] = jnp.where(low, even, pltpu.roll(odd, W, 1))
            rows_ref[b, 1, h] = jnp.where(low, pltpu.roll(even, W, 1), odd)
        for side in range(2):
            for p in range(32):
                given[q, side, :, p * LANES : (p + 1) * LANES] = rows_ref[b, side, :, p, :].astype(BF16)
            put(q, side).start()
    for q in range(4):
        for side in range(2):
            put(q, side).wait()
    if more is not None:
        more.wait()


def finish(*pieces):
    shapes = [jax.ShapeDtypeStruct((8, 8, 4096), BF16)]
    shapes += [jax.ShapeDtypeStruct(piece.shape, piece.dtype) for piece in pieces[6:]]
    specs = [pl.BlockSpec(memory_space=pl.ANY)] * len(shapes)
    return pl.pallas_call(
        finish_kernel,
        out_shape=shapes if len(shapes) > 1 else shapes[0],
        in_specs=[pl.BlockSpec(memory_space=pltpu.VMEM)] * len(pieces),
        out_specs=specs if len(shapes) > 1 else specs[0],
        scratch_shapes=[
            pltpu.VMEM((4, 2, 8, 4096), BF16),
            pltpu.VMEM((2, 8, 64, LANES), F32),
            pltpu.VMEM((2, 2, 8, 32, LANES), F32),
            pltpu.SemaphoreType.DMA((4, 2)),
            pltpu.SemaphoreType.DMA,
        ],
        compiler_params=params(12),
        name="finish",
    )(*pieces)


def listed(position, k):
    odd = lax.rem(position, 2)
    return lax.rem(position + (0, 1 + 2 * odd, 3 - 2 * odd, 2)[k], 4)


def route_kernel(at, b0, b1, b2, b3, o0, o1, o2, o3, held):
    for k, ref in enumerate((b0, b1, b2, b3)):
        held[k] = ref[...]
    for k, ref in enumerate((o0, o1, o2, o3)):
        ref[...] = held[place_of(listed(at[2], k), at[0])]


def route_weights(at, blocks):
    shape = jax.ShapeDtypeStruct((9, 64, LANES), BF16)
    near = pl.BlockSpec(memory_space=pltpu.VMEM)
    return pl.pallas_call(
        route_kernel,
        out_shape=(shape,) * 4,
        in_specs=[pl.BlockSpec(memory_space=pltpu.SMEM)] + [near] * 4,
        out_specs=[near] * 4,
        scratch_shapes=[pltpu.VMEM((4, 9, 64, LANES), BF16)],
        compiler_params=params(4),
        name="route",
    )(at, *blocks)


def weights_kernel(at, mine, other, w_ref, wt_ref, whole):
    core, y = at[1], at[3]
    for ref, side in ((mine, core), (other, 1 - core)):
        lanes = pl.ds(pl.multiple_of(side * LANES, LANES), LANES)
        for k in range(4):
            for tap in range(9):
                whole[tap, k * 64 : (k + 1) * 64, lanes] = ref[k, tap]
    place, channel = row_of((256, 256)), lane_of((256, 256))
    order = jnp.where(
        (place_of(channel // 64, y) == place // 64) & (channel % 64 == place % 64), 1.0, 0.0
    ).astype(BF16)
    across = (((1,), (1,)), ((), ()))
    for tap in range(9):
        straight = lax.dot_general(whole[tap], order, across, preferred_element_type=F32).astype(BF16)
        turned = lax.dot_general(order, whole[tap], across, preferred_element_type=F32).astype(BF16)
        a, c = tap // 3, tap % 3
        w_ref[a, :, c * 256 : (c + 1) * 256] = straight
        wt_ref[2 - a, :, (2 - c) * 256 : (3 - c) * 256] = turned


def arrange_weights(at, mine, other):
    shape = jax.ShapeDtypeStruct((3, 256, 768), BF16)
    return pl.pallas_call(
        weights_kernel,
        out_shape=(shape, shape),
        in_specs=[pl.BlockSpec(memory_space=pltpu.SMEM)] + [pl.BlockSpec(memory_space=pltpu.VMEM)] * 2,
        out_specs=[pl.BlockSpec(memory_space=pltpu.VMEM)] * 2,
        scratch_shapes=[pltpu.VMEM((9, 256, 256), BF16)],
        compiler_params=params(20),
        name="weights",
    )(at, mine, other)


def lay_shifted(q, chunks, top, bottom, rows, shifted):
    column = lane_of((64, LANES)) % W
    not_first = jnp.where(column == 0, 0.0, 1.0).astype(BF16)
    not_last = jnp.where(column == W - 1, 0.0, 1.0).astype(BF16)
    for k in range(4):
        at = k * 64
        for j, h in enumerate(rows):
            if h == -1:
                tile = top[k, q]
            elif h == 8:
                tile = bottom[k, q]
            else:
                tile = chunks[k][q, :, h * LANES : (h + 1) * LANES]
            lanes = slice(j * LANES, (j + 1) * LANES)
            shifted[at : at + 64, lanes] = pltpu.roll(tile, 1, 1) * not_first
            shifted[256 + at : 320 + at, lanes] = tile
            shifted[512 + at : 576 + at, lanes] = pltpu.roll(tile, LANES - 1, 1) * not_last


def conv_kernel(halves, rows, at, c0, c1, c2, c3, *refs):
    edged = 1 in halves
    top, bottom = refs[:2] if edged else (None, None)
    refs = refs[2 * edged :]
    w_ref, both = refs[0], refs[-1]

    def lay(q, shifted):
        lay_shifted(q, (c0, c1, c2, c3), top, bottom, rows, shifted)

    def multiply(q, shifted):
        for i, half in enumerate(halves):
            own, following, send = refs[1 + 3 * i : 4 + 3 * i]
            for n in range(2):
                part = None
                for a in range(3):
                    places = [rows.index(h - 1 + a) for h in ROWS[half][2 * n : 2 * n + 2]]
                    source = jnp.concatenate([shifted[:, j * LANES : (j + 1) * LANES] for j in places], axis=1)
                    term = jnp.dot(w_ref[a], source, preferred_element_type=F32)
                    part = term if part is None else part + term
                lanes = slice(n * 256, (n + 1) * 256)
                own[q, :, lanes] = part[0:64]
                pair = (following.at[q], send.at[0, q]) if half else (send.at[0, q], following.at[q])
                pair[0][:, lanes] = part[64:128]
                pair[1][:, lanes] = part[128:192]
                send[1, q, :, lanes] = part[192:256]

    lay(0, both.at[0])
    for q in range(4):
        if q < 3:
            lay(q + 1, both.at[(q + 1) % 2])
        multiply(q, both.at[q % 2])


def conv(halves, at, chunks, sides, weights):
    rows = {(0,): (0, 1, 2, 3, 4, 5), (1,): (4, 5, 6, 7, 8, -1, 0, 1)}.get(halves, tuple(range(-1, 9)))
    single = jax.ShapeDtypeStruct((4, 64, 512), F32)
    double = jax.ShapeDtypeStruct((2, 4, 64, 512), F32)
    near = pl.BlockSpec(memory_space=pltpu.VMEM)
    sides = sides if 1 in halves else ()
    return pl.pallas_call(
        functools.partial(conv_kernel, halves, rows),
        out_shape=(single, single, double) * len(halves),
        in_specs=[pl.BlockSpec(memory_space=pltpu.SMEM)] + [near] * (5 + len(sides)),
        out_specs=[near] * (3 * len(halves)),
        scratch_shapes=[pltpu.VMEM((2, 768, len(rows) * LANES), BF16)],
        compiler_params=params(20),
        cost_estimate=pl.CostEstimate(
            flops=2415919104 * len(halves), bytes_accessed=6000000 * len(halves), transcendentals=0
        ),
    )(at, *chunks, *sides, weights)


def kernel_grad_kernel(at, x0, x1, x2, x3, top, bottom, g0, g1, g2, g3, mine, other, shifted, grads, total):
    z, core, x, y = at[0], at[1], at[2], at[3]

    def add(q, first):
        lay_shifted(q, (x0, x1, x2, x3), top, bottom, range(-1, 9), shifted)
        for k, g_ref in enumerate((g0, g1, g2, g3)):
            grads[k * 64 : (k + 1) * 64, :] = g_ref[q]
        for a in range(3):
            term = lax.dot_general(
                grads[...],
                shifted[:, a * LANES : a * LANES + 1024],
                (((1,), (1,)), ((), ())),
                preferred_element_type=F32,
            )
            total[a] = term if first else total[a] + term

    add(0, True)

    @pl.loop(1, 4)
    def _(q):
        add(q, False)

    for half, o_ref in ((core, mine), (1 - core, other)):
        second = jnp.where(half == y // 2, 0, 1)
        straight = second == lax.rem(y, 2)
        for k in range(4):
            member = lax.rem(z + (0, 1, 3, 2)[k], 4)
            rows = pl.ds(pl.multiple_of(place_of(member, x) * 64, 64), 64)
            for a in range(3):
                for c in range(3):
                    lanes = pl.ds(pl.multiple_of(c * 256 + second * LANES, LANES), LANES)
                    tile = total[a, rows, lanes]
                    o_ref[k, a * 3 + c] = jnp.where(straight, tile, pltpu.roll(tile, W, 1))


def weight_grads(at, chunks, top, bottom, grads):
    shape = jax.ShapeDtypeStruct((4, 9, 64, LANES), F32)
    near = pl.BlockSpec(memory_space=pltpu.VMEM)
    return pl.pallas_call(
        kernel_grad_kernel,
        out_shape=(shape,) * 2,
        in_specs=[pl.BlockSpec(memory_space=pltpu.SMEM)] + [near] * 10,
        out_specs=[near] * 2,
        scratch_shapes=[pltpu.VMEM((768, 1280), BF16), pltpu.VMEM((256, 1024), BF16), pltpu.VMEM((3, 256, 768), F32)],
        compiler_params=params(20),
        cost_estimate=pl.CostEstimate(flops=4831838208, bytes_accessed=9000000, transcendentals=0),
        name="weight_grads",
    )(at, *chunks, top, bottom, *grads)


def ring(step):
    return [(i, (i + step) % 4) for i in range(4)]


def after(value, *others):
    return lax.optimization_barrier((value, *others))[0]


def gather(block, axis):
    return (
        block, lax.ppermute(block, axis, FIRST), lax.ppermute(block, axis, SECOND), lax.ppermute(block, axis, OPPOSITE)
    )


def edges(chunks):
    forward = [(i, i + 1) for i in range(7)]
    backward = [(j, i) for i, j in forward]
    last = jnp.stack([chunk[:, :, -LANES:] for chunk in chunks])
    first = jnp.stack([chunk[:, :, :LANES] for chunk in chunks])
    return (lax.ppermute(last, ("z", "core"), forward), lax.ppermute(first, ("z", "core"), backward))


def reduce_second(a, b, one_a, one_b, axis):
    two_a = lax.ppermute(a[1] + one_a[1], axis, SECOND)
    two_b = lax.ppermute(b[1] + one_b[1], axis, FIRST)
    return a[0], one_a, two_a, b[0], one_b, two_b


def fetch_weights(at, block):
    along_z = gather(block, "z")
    own, first, second, far = route_weights(at, along_z)
    got = (own, lax.ppermute(first, "x", FIRST), lax.ppermute(second, "x", SECOND), lax.ppermute(far, "x", OPPOSITE))
    got = jnp.stack(got)
    other = lax.ppermute(got, "core", SWAP)
    return arrange_weights(at, got, other)


def step(images, kernel, upstream):
    at = jnp.stack([lax.axis_index(n) for n in ("z", "core", "x", "y")]).astype(jnp.int32)
    weights, turned = fetch_weights(at, kernel.reshape(9, 64, LANES))
    x, g = pack(images, upstream)
    x_chunks = gather(x, "y")
    g_chunks = gather(g, "x")

    x_sides = edges(x_chunks)
    g_sides = edges(g_chunks)
    out_a = conv((0,), at, x_chunks, x_sides, weights)
    out_one_a = lax.ppermute(out_a[2], "x", FIRST)
    out_b = conv((1,), after(at, out_a[0]), x_chunks, x_sides, weights)
    out_one_b = lax.ppermute(out_b[2], "x", SECOND)
    grad_a = conv((0,), after(at, out_b[0]), g_chunks, g_sides, turned)
    grad_one_a = lax.ppermute(grad_a[2], "y", FIRST)
    grad_b = conv((1,), after(at, grad_a[0]), g_chunks, g_sides, turned)
    grad_one_b = lax.ppermute(grad_b[2], "y", SECOND)

    near, far = weight_grads(after(at, grad_b[0]), x_chunks, *x_sides, g_chunks)
    near = near + lax.ppermute(far, "core", SWAP)
    output_maps = finish(*reduce_second(out_a, out_b, out_one_a, out_one_b, "x"))
    grad_pieces = reduce_second(grad_a, grad_b, grad_one_a, grad_one_b, "y")
    total = near[0]
    for k, turn in ((1, 1), (2, 3), (3, 2)):
        total = total + lax.ppermute(near[k], "z", ring(turn))
    cross = [(z * 4 + x, x * 4 + z) for z in range(4) for x in range(4)]
    home = lax.ppermute(total, ("z", "x"), cross)
    input_grad, kernel_grad = finish(*grad_pieces, home)
    return output_maps, input_grad, kernel_grad.reshape(3, 3, 64, LANES)


def solution(mesh):
    fine = Mesh(mesh.devices.reshape(4, 2, 4, 4), ("z", "core", "x", "y"))
    row, col = ("z", "core"), ("x", "y")
    flat = P(None, row, col)
    taps = P(None, None, col, row)
    return jax.shard_map(step, mesh=fine, in_specs=(flat, taps, flat), out_specs=(flat, flat, taps), check_vma=False)
```
